512 devices in a mesh: sub: 16 (over z_lo, x), reg: 32 (over y, z_hi, core).
Axes of the slice: x: 4, y: 8, z: 8 (z_hi: 2, z_lo: 4; z = z_hi * 4 + z_lo), core: 2. Of those that a mesh axis runs over, the one named last changes fastest.
Arguments:
- port_loads: bfloat16 [32, 16, 384, 512], P('reg', 'sub'), may hold values from -6 to 6
- leaf_inverse: bfloat16 [32, 16, 384, 384], P('reg', 'sub'), may hold values from -3 to 3, as said below
- leaf_coupling: bfloat16 [32, 16, 896, 384], P('reg', 'sub'), may hold values from -0.3125 to 0.3125
- first_inverse: bfloat16 [32, 7168, 896], P('reg', 'sub'), may hold values from -3 to 3, as said below
- second_coupling: bfloat16 [32, 7168, 896], P('reg', 'sub'), may hold values from -0.1875 to 0.1875
- second_inverse: bfloat16 [32, 3584, 896], P('reg', 'sub'), may hold values from -3 to 3, as said below
- border_coupling: bfloat16 [32, 2048, 896], P('reg', 'sub'), may hold values from -0.1875 to 0.1875
- border_inverse: bfloat16 [512, 512], replicated, may hold values from -3 to 3, as said below
- border_rows: int32 [32], P('reg'), may hold values from 128 to 512, as said below
Outputs:
- solution: bfloat16 [32, 16, 384, 512], P('reg', 'sub')
The draws below stay inside these ranges and needn't reach their ends.
Inputs may be any that keep to these rules, and one draw needn't show every extreme that they name: `leaf_inverse`: every 384 x 384 block is lower triangular. `first_inverse`: every 896 x 896 block is lower triangular. `second_inverse`: every 896 x 896 block is lower triangular. `border_inverse`: lower triangular. `border_rows`: some region touches all 512 rows.
All inputs are finite; a program needn't handle non-finite values.
Results may differ from the reference program's by a relative error of at most 0.013.
Values may be sent and summed in bfloat16 or wider, within the bound.
No kernel may reach another device: no remote copies, remote signals or barrier semaphores. Data moves between devices by JAX's collectives and lax.ppermute only.
A program may use at most 64 MiB of HBM per device.

```python
import math
import jax
import jax.numpy as jnp
from jax import lax

P_SIZE = 512
SEP = 896
BORDER = 512
LEAF = 384
TOP_SEPS = 128
N_SUB = 16
N_REG = 32


def lower_blocks(key, count, order, factor):
    noise_key, diag_key = jax.random.split(key, 2)
    noise = jnp.clip(jax.random.normal(noise_key, (count, order, order), jnp.float32), -4.0, 4.0) * 0.7
    diagonal = jnp.exp(jax.random.uniform(diag_key, (count, order), jnp.float32, math.log(0.5), math.log(2.0)))
    lower = jnp.tril(noise, -1) / math.sqrt(order)
    identity = jnp.eye(order, dtype=jnp.float32)
    return factor * (lower + diagonal[:, :, None] * identity)


def draw_leaf_inverse(key, part):
    blocks = lower_blocks(jax.random.fold_in(key, 101), N_REG * N_SUB, LEAF, 1.0)
    return blocks.reshape(N_REG, N_SUB, LEAF, LEAF).astype(jnp.bfloat16)


def draw_first_inverse(key, part):
    blocks = lower_blocks(jax.random.fold_in(key, 102), N_REG * (N_SUB // 2), SEP, 1.0)
    return blocks.reshape(N_REG, N_SUB // 2 * SEP, SEP).astype(jnp.bfloat16)


def draw_second_inverse(key, part):
    blocks = lower_blocks(jax.random.fold_in(key, 103), N_REG * (N_SUB // 4), SEP, 1.0)
    return blocks.reshape(N_REG, N_SUB // 4 * SEP, SEP).astype(jnp.bfloat16)


def draw_border_inverse(key, part):
    factor = math.sqrt(0.5) * (BORDER * TOP_SEPS / SEP) ** (-0.25)
    blocks = lower_blocks(jax.random.fold_in(key, 104), 1, BORDER, factor)
    return blocks.reshape(BORDER, BORDER).astype(jnp.bfloat16)


def draw_border_rows(key, part):
    value_key, pick_key = jax.random.split(jax.random.fold_in(key, 105), 2)
    values = jax.random.randint(value_key, (N_REG,), BORDER // 4, BORDER + 1, dtype=jnp.int32)
    chosen = jax.random.randint(pick_key, (), 0, N_REG, dtype=jnp.int32)
    return values.at[chosen].set(BORDER)


def shard_levels(rng, extent, cuts, low, top_value):
    level = 1.0
    for axis_at, blocks in cuts:
        heights = jax.random.uniform(jax.random.fold_in(jax.random.fold_in(rng, 6), axis_at), (blocks,), jnp.float32, low / len(cuts), top_value / len(cuts))
        level = level * jnp.repeat(jnp.exp(heights), extent[axis_at] // blocks).reshape((-1,) + (1,) * (len(extent) - 1 - axis_at))
    return level


def scatter_about(rng, dims, deviation, reach, pieces=(), kind=jnp.bfloat16):
    values = deviation * jax.random.normal(rng, dims, jnp.float32)
    if pieces:
        values = values * shard_levels(rng, dims, pieces, -0.22, 0.18)
    return jnp.clip(values, -reach, reach).astype(kind)


def setup_inputs(seed: int = 0) -> dict:
    arg_keys = jax.random.split(jax.random.key(seed), 10)
    port_loads = scatter_about(arg_keys[0], (N_REG, N_SUB, LEAF, P_SIZE), 1.0, 6.0, ((0, 32), (1, 16)))
    leaf_inverse = draw_leaf_inverse(jax.random.fold_in(arg_keys[9], 71), 0)
    leaf_coupling = scatter_about(arg_keys[2], (N_REG, N_SUB, SEP, LEAF), LEAF ** -0.5, 0.3125, ((0, 32), (1, 16)))
    first_inverse = draw_first_inverse(jax.random.fold_in(arg_keys[9], 71), 0)
    second_coupling = scatter_about(arg_keys[4], (N_REG, N_SUB // 2 * SEP, SEP), SEP ** -0.5, 0.1875, ((0, 32), (1, 16)))
    second_inverse = draw_second_inverse(jax.random.fold_in(arg_keys[9], 71), 0)
    border_coupling = scatter_about(arg_keys[6], (N_REG, N_SUB // 4 * BORDER, SEP), SEP ** -0.5, 0.1875, ((0, 32), (1, 16)))
    border_inverse = draw_border_inverse(jax.random.fold_in(arg_keys[9], 71), 0)
    border_rows = draw_border_rows(jax.random.fold_in(arg_keys[9], 71), 0)
    return dict(port_loads=port_loads, leaf_inverse=leaf_inverse, leaf_coupling=leaf_coupling, first_inverse=first_inverse, second_coupling=second_coupling, second_inverse=second_inverse, border_coupling=border_coupling, border_inverse=border_inverse, border_rows=border_rows)


def widen(array):
    return array.astype(jnp.float32)


def reference(port_loads, leaf_inverse, leaf_coupling, first_inverse, second_coupling, second_inverse, border_coupling, border_inverse, border_rows):
    def forward(region_data):
        loads, leaf_inv, leaf_coup, inv_one, coup_two, inv_two, coup_border, live_rows = region_data
        fwd_leaf = jnp.einsum('sij,sjp->sip', widen(leaf_inv), widen(loads)).astype(jnp.bfloat16)
        part_one = jnp.einsum('sij,sjp->sip', widen(leaf_coup), widen(fwd_leaf)).reshape(N_SUB // 2, 2, SEP, P_SIZE)
        rhs_one = (-(part_one[:, 0] + part_one[:, 1])).astype(jnp.bfloat16)
        inv_one = inv_one.reshape(N_SUB // 2, SEP, SEP)
        coup_two = coup_two.reshape(N_SUB // 2, SEP, SEP)
        fwd_one = jnp.einsum('sij,sjp->sip', widen(inv_one), widen(rhs_one)).astype(jnp.bfloat16)
        part_two = jnp.einsum('sij,sjp->sip', widen(coup_two), widen(fwd_one)).reshape(N_SUB // 4, 2, SEP, P_SIZE)
        rhs_two = (-(part_two[:, 0] + part_two[:, 1])).astype(jnp.bfloat16)
        inv_two = inv_two.reshape(N_SUB // 4, SEP, SEP)
        fwd_two = jnp.einsum('sij,sjp->sip', widen(inv_two), widen(rhs_two)).astype(jnp.bfloat16)
        coup_border = coup_border.reshape(N_SUB // 4, BORDER, SEP)
        row_mask = (jnp.arange(BORDER, dtype=jnp.int32) < live_rows)[:, None]
        part_border = jnp.einsum('sij,sjp->sip', widen(coup_border), widen(fwd_two))
        part_border = jnp.where(row_mask[None], part_border, jnp.float32(0.0))
        return fwd_leaf, fwd_one, fwd_two, jnp.sum(part_border, axis=0)

    fwd_leaf, fwd_one, fwd_two, region_parts = lax.map(forward, (port_loads, leaf_inverse, leaf_coupling, first_inverse, second_coupling, second_inverse, border_coupling, border_rows))
    rhs_border = (-jnp.sum(region_parts, axis=0)).astype(jnp.bfloat16)
    fwd_border = jnp.dot(border_inverse, rhs_border, preferred_element_type=jnp.float32).astype(jnp.bfloat16)
    back_border = jnp.dot(border_inverse.T, fwd_border, preferred_element_type=jnp.float32).astype(jnp.bfloat16)

    def backward(region_data):
        leaf_fwd, one_fwd, two_fwd, leaf_inv, leaf_coup, inv_one, coup_two, inv_two, coup_border, live_rows = region_data
        row_mask = (jnp.arange(BORDER, dtype=jnp.int32) < live_rows)[:, None]
        masked = jnp.where(row_mask, widen(back_border), jnp.float32(0.0))
        coup_border = coup_border.reshape(N_SUB // 4, BORDER, SEP)
        diff_two = (widen(two_fwd) - jnp.einsum('sij,ip->sjp', widen(coup_border), masked)).astype(jnp.bfloat16)
        inv_two = inv_two.reshape(N_SUB // 4, SEP, SEP)
        back_two = jnp.einsum('sji,sjp->sip', widen(inv_two), widen(diff_two)).astype(jnp.bfloat16)
        parent_two = jnp.repeat(back_two, 2, axis=0)
        coup_two = coup_two.reshape(N_SUB // 2, SEP, SEP)
        diff_one = (widen(one_fwd) - jnp.einsum('sji,sjp->sip', widen(coup_two), widen(parent_two))).astype(jnp.bfloat16)
        inv_one = inv_one.reshape(N_SUB // 2, SEP, SEP)
        back_one = jnp.einsum('sji,sjp->sip', widen(inv_one), widen(diff_one)).astype(jnp.bfloat16)
        parent_one = jnp.repeat(back_one, 2, axis=0)
        diff_leaf = (widen(leaf_fwd) - jnp.einsum('sji,sjp->sip', widen(leaf_coup), widen(parent_one))).astype(jnp.bfloat16)
        return jnp.einsum('sji,sjp->sip', widen(leaf_inv), widen(diff_leaf)).astype(jnp.bfloat16)

    return lax.map(backward, (fwd_leaf, fwd_one, fwd_two, leaf_inverse, leaf_coupling, first_inverse, second_coupling, second_inverse, border_coupling, border_rows))
```

```python
import jax
import jax.numpy as jnp
from jax import lax
from jax.sharding import PartitionSpec as P


from jax.sharding import Mesh

AXES = ("zl", "x", "y", "zh", "c")
GROUP = ("zl", "y", "zh", "c")
NEAR = [(0, 1), (1, 0), (2, 3), (3, 2)]
NEXT = [(0, 3), (3, 0), (1, 2), (2, 1)]
BF = jnp.bfloat16


def send(x, pairs):
    return lax.ppermute(x, "x", pairs)


def to_group(tiles):
    return lax.all_to_all(tiles, GROUP, split_axis=0, concat_axis=0, tiled=True)


def attach(mine, other, mine_first, axis_pos):
    return jnp.where(
        mine_first,
        jnp.concatenate([mine, other], axis_pos),
        jnp.concatenate([other, mine], axis_pos),
    )


def apply_transpose(matrix, vector):
    return lax.dot_general(
        matrix, vector, (((0,), (0,)), ((), ())), preferred_element_type=jnp.float32
    )


def product(matrix, vector):
    return jnp.dot(matrix, vector, preferred_element_type=jnp.float32)


def per_device(
    port_loads,
    leaf_inverse,
    leaf_coupling,
    first_inverse,
    second_coupling,
    second_inverse,
    border_coupling,
    border_inverse,
    border_rows,
):
    at = lax.axis_index("x")
    low = at % 2 == 0
    first_half = (at == 0) | (at == 3)
    lower = at < 2
    group = lax.axis_size(GROUP)
    leaf_inv = leaf_inverse[0, 0]
    leaf_coup = leaf_coupling[0, 0]
    fwd_leaf = product(leaf_inv, port_loads[0, 0]).astype(BF)
    half = fwd_leaf.shape[1] // 2
    left, right = fwd_leaf[:, :half], fwd_leaf[:, half:]
    sent_one = product(leaf_coup, jnp.where(first_half, right, left)).astype(BF)
    came_one = send(sent_one, NEAR)
    inv_one = first_inverse[0]
    coup_two = second_coupling[0]
    inv_two = second_inverse[0]
    coup_border = border_coupling[0]
    inv_one = attach(inv_one, send(inv_one, NEAR), low, 0)
    inv_two = attach(inv_two, send(inv_two, NEAR), low, 0)
    coup_border = attach(coup_border, send(coup_border, NEAR), low, 0)
    coup_two = attach(coup_two, send(coup_two, NEAR), low, 0)
    inv_two = attach(inv_two, send(inv_two, NEXT), lower, 0)
    coup_border = attach(coup_border, send(coup_border, NEXT), lower, 0)
    kept_one = product(leaf_coup, jnp.where(first_half, left, right))
    rhs_one = (-(kept_one + came_one.astype(jnp.float32))).astype(BF)
    fwd_one = product(inv_one, rhs_one).astype(BF)
    part_two = product(coup_two, fwd_one)
    quarter = half // 2
    kept_two = jnp.where(lower, part_two[:, :quarter], part_two[:, quarter:])
    sent_two = jnp.where(lower, part_two[:, quarter:], part_two[:, :quarter])
    came_two = send(sent_two.astype(BF), NEXT)
    rhs_two = (-(kept_two + came_two.astype(jnp.float32))).astype(BF)
    fwd_two = product(inv_two, rhs_two).astype(BF)
    border_count = coup_border.shape[0]
    row_mask = lax.broadcasted_iota(jnp.int32, (border_count, 1), 0) < border_rows[0]
    part_border = jnp.where(row_mask, product(coup_border, fwd_two), jnp.float32(0.0))
    tiles = part_border.astype(BF).reshape(group, border_count // group, quarter)
    share_sum = jnp.sum(to_group(tiles).astype(jnp.float32), axis=0)
    rhs_share = (-share_sum).astype(BF)
    rhs_border = to_group(jnp.broadcast_to(rhs_share, tiles.shape)).reshape(border_count, quarter)
    fwd_border = product(border_inverse, rhs_border).astype(BF)
    back_border = apply_transpose(border_inverse, fwd_border).astype(BF)
    masked = jnp.where(row_mask, back_border, jnp.zeros_like(back_border))
    diff_two = (fwd_two.astype(jnp.float32) - apply_transpose(coup_border, masked)).astype(BF)
    back_two = apply_transpose(inv_two, diff_two).astype(BF)
    back_two = attach(back_two, send(back_two, NEXT), lower, 1)
    diff_one = (fwd_one.astype(jnp.float32) - apply_transpose(coup_two, back_two)).astype(BF)
    back_one = apply_transpose(inv_one, diff_one).astype(BF)
    back_one = attach(back_one, send(back_one, NEAR), first_half, 1)
    diff_leaf = (fwd_leaf.astype(jnp.float32) - apply_transpose(leaf_coup, back_one)).astype(BF)
    solution = apply_transpose(leaf_inv, diff_leaf).astype(BF)
    return solution[None, None]


def solution(mesh):
    split = Mesh(mesh.devices.reshape(4, 4, 8, 2, 2), AXES)
    reg, sub = ("y", "zh", "c"), ("zl", "x")
    return jax.shard_map(
        per_device,
        mesh=split,
        in_specs=(P(reg, sub),) * 7 + (P(None, None), P(reg)),
        out_specs=P(reg, sub),
        check_vma=False,
    )
```

```python
import jax
import jax.numpy as jnp
from jax import lax
from jax.experimental import pallas as pl
from jax.experimental.pallas import tpu as pltpu
from jax.sharding import Mesh
from jax.sharding import PartitionSpec as P


AXES = ("zl", "x", "y", "zh", "c")
GROUP = ("zl", "y", "zh", "c")
NEAR = [(0, 1), (1, 0), (2, 3), (3, 2)]
NEXT = [(0, 3), (3, 0), (1, 2), (2, 1)]
ACROSS = [(0, 2), (2, 0), (1, 3), (3, 1)]
DOWN = [(0, 1), (2, 3)]
BF = jnp.bfloat16
F32 = jnp.float32

LANES = 128


def send(x, pairs):
    return lax.ppermute(x, "x", pairs)


def to_group(tiles):
    return lax.all_to_all(tiles, GROUP, split_axis=0, concat_axis=0, tiled=True)


def mul(a, b):
    return jnp.dot(a, b, preferred_element_type=F32)


def mul_t(a, b):
    return lax.dot_general(a, b, (((0,), (0,)), ((), ())), preferred_element_type=F32)


def call(kernel, outs, scratch, *args, flops=0):
    moved = sum(a.size * a.dtype.itemsize for a in args)
    space = pl.BlockSpec(memory_space=pltpu.VMEM)
    return pl.pallas_call(
        kernel,
        out_shape=[jax.ShapeDtypeStruct(s, d) for s, d in outs],
        in_specs=[
            pl.BlockSpec(memory_space=pltpu.SMEM) if a.dtype == jnp.int32 else space
            for a in args
        ],
        out_specs=[space] * len(outs),
        scratch_shapes=[pltpu.VMEM(s, d) for s, d in scratch],
        compiler_params=pltpu.CompilerParams(vmem_limit_bytes=24 << 20),
        cost_estimate=pl.CostEstimate(flops=flops, bytes_accessed=moved, transcendentals=0),
    )(*args)


def others(x):
    return x ^ 1, 3 - x, x ^ 2


def leaf_kernel(loads, inv, coup, fwd, top, bot):
    fwd[...] = mul(inv[...], loads[...]).astype(BF)
    half = top.shape[0]
    top[...] = mul(coup[:half], fwd[...]).astype(BF)
    bot[...] = mul(coup[half:], fwd[...]).astype(BF)


def first_kernel(at, inv, top, bot, came_top, came_bot, coup, came_coup, pack, own, near, nxt, far, rhs, held):
    x = at[0]
    high = x % 2
    half, sep = inv.shape
    ports = top.shape[1]
    width = held.shape[0]
    rhs[:half] = (-(top[...].astype(F32) + came_top[...].astype(F32))).astype(BF)
    rhs[half:] = (-(bot[...].astype(F32) + came_bot[...].astype(F32))).astype(BF)
    fwd = mul(inv[...], rhs[...]).astype(BF)
    pack[:, :sep] = inv[...]
    pack[:, sep + sep - width :] = fwd
    pad = width - half
    held[:pad] = jnp.zeros((pad, ports), BF)
    held[half:] = jnp.zeros((pad, ports), BF)
    start = pl.multiple_of(high * pad, pad)
    held[pl.ds(start, half)] = fwd
    lane = pl.multiple_of(high * (sep - width), LANES)
    rest = pl.multiple_of(high * width, LANES)
    pack[:, sep : sep + sep - width] = coup[:, pl.ds(rest, sep - width)]
    mine = coup[:, pl.ds(lane, width)]
    mine_at = pl.multiple_of(high * half, half)
    other_at = pl.multiple_of((1 - high) * half, half)
    share = own.shape[1]
    for ref, who in zip((far, nxt, near, own), others(x)[::-1] + (x,)):
        cols = held[:, pl.ds(pl.multiple_of(who * share, LANES), share)]
        ref[pl.ds(mine_at, half)] = mul(mine, cols).astype(BF)
        ref[pl.ds(other_at, half)] = mul(came_coup[...], cols).astype(BF)


def pieces(x, refs):
    return zip((x,) + others(x), refs)


def second_kernel(at, rows, own, near, nxt, far, w0, w1, w2, w3, fwd, tiles, rhs):
    x = at[0]
    total = own[...].astype(F32) + near[...].astype(F32)
    total = total + (nxt[...].astype(F32) + far[...].astype(F32))
    rhs[...] = (-total).astype(BF)
    each = rhs.shape[0] // 4
    for who, ref in pieces(x, (w0, w1, w2, w3)):
        fwd[pl.ds(pl.multiple_of(who * each, each), each)] = mul(ref[:each], rhs[...]).astype(BF)
    for who, ref in pieces(x, (w0, w1, w2, w3)):
        count = ref.shape[0] - each
        first = pl.multiple_of(who * count, count)
        part = mul(ref[each:], fwd[...])
        live = lax.broadcasted_iota(jnp.int32, part.shape, 0) + first < rows[0]
        tiles[pl.ds(first, count)] = jnp.where(live, part, 0.0).astype(BF)


def border_kernel(at, rows, rhs, inv, fwd, w0, w1, w2, w3, back, sol):
    x = at[0]
    mid = mul(inv[...], rhs[...]).astype(BF)
    end = mul_t(inv[...], mid)
    live = lax.broadcasted_iota(jnp.int32, end.shape, 0) < rows[0]
    sol[...] = jnp.where(live, end, 0.0).astype(BF)
    each = fwd.shape[0] // 4
    diff = fwd[...].astype(F32)
    for who, ref in pieces(x, (w0, w1, w2, w3)):
        count = ref.shape[0] - each
        diff = diff - mul_t(ref[each:], sol[pl.ds(pl.multiple_of(who * count, count), count)])
    fwd_ref = back
    fwd_ref[...] = diff.astype(BF)
    total = None
    for who, ref in pieces(x, (w0, w1, w2, w3)):
        term = mul_t(ref[:each], fwd_ref[pl.ds(pl.multiple_of(who * each, each), each)])
        total = term if total is None else total + term
    back[...] = total.astype(BF)


def fold_kernel(at, pack, came, coup, came_coup, leaf_coup, fwd_leaf, fold, rest, full):
    high = at[0] % 2
    half, sep = coup.shape
    width = came_coup.shape[1]
    mine_at = pl.multiple_of(high * half, half)
    other_at = pl.multiple_of((1 - high) * half, half)
    mine = mul(pack[:, :sep], leaf_coup[...]).astype(BF)
    other = mul(came[:, :sep], leaf_coup[...]).astype(BF)
    full[pl.ds(mine_at, half)] = mine
    full[pl.ds(other_at, half)] = other
    rest[...] = (
        fwd_leaf[...].astype(F32)
        - mul_t(mine, pack[:, sep + sep - width :])
        - mul_t(other, came[:, sep + sep - width :])
    )
    fold[pl.ds(mine_at, half)] = mul(coup[...], full[...]).astype(BF)
    win = pl.multiple_of(high * (sep - width), LANES)
    out = pl.multiple_of((1 - high) * width, LANES)
    fold[pl.ds(other_at, half)] = (
        mul(came_coup[...], full[pl.ds(win, width)])
        + mul(came[:, sep : sep + sep - width], full[pl.ds(out, sep - width)])
    ).astype(BF)


def last_kernel(at, fold, rest, own, near, nxt, far, inv, out, diff):
    share = own.shape[1]
    for who, ref in pieces(at[0], (own, near, nxt, far)):
        cols = pl.ds(pl.multiple_of(who * share, LANES), share)
        diff[:, cols] = (rest[:, cols] + mul_t(fold[...], ref[...])).astype(BF)
    out[...] = mul_t(inv[...], diff[...]).astype(BF)


def per_device(
    port_loads,
    leaf_inverse,
    leaf_coupling,
    first_inverse,
    second_coupling,
    second_inverse,
    border_coupling,
    border_inverse,
    border_rows,
):
    x = lax.axis_index("x")
    at = x.astype(jnp.int32)[None]
    low = x % 2 == 0
    group = lax.axis_size(GROUP)
    loads, leaf_inv, leaf_coup = port_loads[0, 0], leaf_inverse[0, 0], leaf_coupling[0, 0]
    inv_one, coup_two = first_inverse[0], second_coupling[0]
    half, sep = inv_one.shape
    leaf, ports = loads.shape
    share = ports // 4
    width = -(-half // LANES) * LANES
    border = border_inverse.shape[0]

    window = jnp.where(low, coup_two[:, sep - width :], coup_two[:, :width])
    came_coup = send(window, NEAR)
    block = jnp.concatenate([second_inverse[0], border_coupling[0]], 0)
    w_next = send(block, NEXT)
    fwd_leaf, top, bot = call(
        leaf_kernel,
        [((leaf, ports), BF), ((half, ports), BF), ((half, ports), BF)],
        [],
        loads,
        leaf_inv,
        leaf_coup,
        flops=2 * leaf * ports * (leaf + sep),
    )
    came_top = send(top, NEAR)
    came_bot = send(bot, DOWN)
    late_block, came_top = lax.optimization_barrier((block, came_top))
    w_near = send(late_block, NEAR)
    w_far = send(w_near, NEXT)
    quarter = ((sep, share), BF)
    pack, own, near, nxt, far = call(
        first_kernel,
        [((half, 2 * sep - width + ports), BF)] + [quarter] * 4,
        [((sep, ports), BF), ((width, ports), BF)],
        at,
        inv_one,
        top,
        bot,
        came_top,
        came_bot,
        coup_two,
        came_coup,
        flops=2 * half * ports * sep + 2 * sep * ports * width,
    )
    far = send(far, ACROSS)
    nxt = send(nxt, NEXT)
    near = send(near, NEAR)
    late_pack, near = lax.optimization_barrier((pack, near))
    came_pack = send(late_pack, NEAR)
    blocks = (block, w_near, w_next, w_far)
    fwd_two, tiles = call(
        second_kernel,
        [quarter, ((border, share), BF)],
        [quarter],
        at,
        border_rows,
        own,
        near,
        nxt,
        far,
        *blocks,
        flops=2 * sep * share * (sep + border),
    )
    tiles = tiles.reshape(group, border // group, share)
    share_sum = jnp.sum(to_group(tiles).astype(F32), axis=0)
    rhs_share = (-share_sum).astype(BF)
    rhs_border = to_group(jnp.broadcast_to(rhs_share, tiles.shape)).reshape(border, share)
    (back_two,) = call(
        border_kernel,
        [quarter],
        [((border, share), BF)],
        at,
        border_rows,
        rhs_border,
        border_inverse,
        fwd_two,
        *blocks,
        flops=2 * share * (2 * border * border + border * sep + sep * sep),
    )
    back_far = send(back_two, ACROSS)
    back_next = send(back_two, NEXT)
    back_near = send(back_two, NEAR)
    pack, came_pack, back_two = lax.optimization_barrier((pack, came_pack, back_two))
    fold, rest = call(
        fold_kernel,
        [((sep, leaf), BF), ((leaf, ports), F32)],
        [((sep, leaf), BF)],
        at,
        pack,
        came_pack,
        coup_two,
        came_coup,
        leaf_coup,
        fwd_leaf,
        flops=2 * sep * leaf * (2 * sep + ports),
    )
    (out,) = call(
        last_kernel,
        [((leaf, ports), BF)],
        [((leaf, ports), BF)],
        at,
        fold,
        rest,
        back_two,
        back_near,
        back_next,
        back_far,
        leaf_inv,
        flops=2 * leaf * ports * (sep + leaf),
    )
    return out[None, None]


def solution(mesh):
    split = Mesh(mesh.devices.reshape(4, 4, 8, 2, 2), AXES)
    reg, sub = ("y", "zh", "c"), ("zl", "x")
    return jax.shard_map(
        per_device,
        mesh=split,
        in_specs=(P(reg, sub),) * 7 + (P(None, None), P(reg)),
        out_specs=P(reg, sub),
        check_vma=False,
    )
```

```python
import jax
import jax.numpy as jnp
from jax import lax
from jax.experimental import pallas as pl
from jax.experimental.pallas import tpu as pltpu
from jax.sharding import Mesh
from jax.sharding import PartitionSpec as P


AXES = ("zl", "x", "y", "zh", "c")
GROUP = ("zl", "y", "zh", "c")
NEAR = [(0, 1), (1, 0), (2, 3), (3, 2)]
NEXT = [(0, 3), (3, 0), (1, 2), (2, 1)]
ACROSS = [(0, 2), (2, 0), (1, 3), (3, 1)]
DOWN = [(0, 1), (2, 3)]
BF = jnp.bfloat16
F32 = jnp.float32

LANES = 128


def send(x, pairs):
    return lax.ppermute(x, "x", pairs)


def to_group(tiles):
    return lax.all_to_all(tiles, GROUP, split_axis=0, concat_axis=0, tiled=True)


def mul(a, b):
    return jnp.dot(a, b, preferred_element_type=F32)


def mul_t(a, b):
    return lax.dot_general(a, b, (((0,), (0,)), ((), ())), preferred_element_type=F32)


def call(kernel, outs, scratch, *args, flops=0):
    moved = sum(a.size * a.dtype.itemsize for a in args)
    space = pl.BlockSpec(memory_space=pltpu.VMEM)
    return pl.pallas_call(
        kernel,
        out_shape=[jax.ShapeDtypeStruct(s, d) for s, d in outs],
        in_specs=[
            pl.BlockSpec(memory_space=pltpu.SMEM) if a.dtype == jnp.int32 else space
            for a in args
        ],
        out_specs=[space] * len(outs),
        scratch_shapes=[pltpu.VMEM(s, d) for s, d in scratch],
        compiler_params=pltpu.CompilerParams(vmem_limit_bytes=24 << 20),
        cost_estimate=pl.CostEstimate(flops=flops, bytes_accessed=moved, transcendentals=0),
    )(*args)


def others(x):
    return x ^ 1, 3 - x, x ^ 2


def leaf_kernel(loads, inv, coup, fwd, top, bot):
    fwd[...] = mul(inv[...], loads[...]).astype(BF)
    half = top.shape[0]
    top[...] = mul(coup[:half], fwd[...]).astype(BF)
    bot[...] = mul(coup[half:], fwd[...]).astype(BF)


def first_kernel(at, inv, top, bot, came_top, came_bot, coup, came_coup, pack, own, near, nxt, far, rhs, held, turned):
    x = at[0]
    high = x % 2
    half, sep = inv.shape
    ports = top.shape[1]
    width = held.shape[0]
    rhs[:half] = (-(top[...].astype(F32) + came_top[...].astype(F32))).astype(BF)
    rhs[half:] = (-(bot[...].astype(F32) + came_bot[...].astype(F32))).astype(BF)
    fwd = mul(inv[...], rhs[...]).astype(BF)
    pack[:, :sep] = inv[...]
    pack[:, sep + sep - width :] = fwd
    pad = width - half
    held[:pad] = jnp.zeros((pad, ports), BF)
    held[half:] = jnp.zeros((pad, ports), BF)
    start = pl.multiple_of(high * pad, pad)
    held[pl.ds(start, half)] = fwd
    lane = pl.multiple_of(high * (sep - width), LANES)
    rest = pl.multiple_of(high * width, LANES)
    pack[:, sep : sep + sep - width] = coup[:, pl.ds(rest, sep - width)]
    mine = coup[:, pl.ds(lane, width)]
    mine_at = pl.multiple_of(high * half, half)
    other_at = pl.multiple_of((1 - high) * half, half)
    share = own.shape[1]
    for at_col, who in enumerate((x,) + others(x)):
        cols = pl.ds(pl.multiple_of(who * share, LANES), share)
        turned[:, at_col * share : (at_col + 1) * share] = held[:, cols]
    for weights, row in ((mine, mine_at), (came_coup[...], other_at)):
        part = mul(weights, turned[...]).astype(BF)
        for at_col, ref in enumerate((own, near, nxt, far)):
            ref[pl.ds(row, half)] = part[:, at_col * share : (at_col + 1) * share]


def pieces(x, refs):
    return zip((x,) + others(x), refs)


def second_kernel(at, rows, own, near, nxt, far, w0, w1, w2, w3, fwd, tiles, rhs):
    x = at[0]
    total = own[...].astype(F32) + near[...].astype(F32)
    total = total + (nxt[...].astype(F32) + far[...].astype(F32))
    rhs[...] = (-total).astype(BF)
    each = rhs.shape[0] // 4
    for who, ref in pieces(x, (w0, w1, w2, w3)):
        fwd[pl.ds(pl.multiple_of(who * each, each), each)] = mul(ref[:each], rhs[...]).astype(BF)
    for who, ref in pieces(x, (w0, w1, w2, w3)):
        count = ref.shape[0] - each
        first = pl.multiple_of(who * count, count)
        part = mul(ref[each:], fwd[...])
        live = lax.broadcasted_iota(jnp.int32, part.shape, 0) + first < rows[0]
        tiles[pl.ds(first, count)] = jnp.where(live, part, 0.0).astype(BF)


def border_kernel(at, rows, rhs, inv, fwd, w0, w1, w2, w3, back, sol):
    x = at[0]
    mid = mul(inv[...], rhs[...]).astype(BF)
    end = mul_t(inv[...], mid)
    live = lax.broadcasted_iota(jnp.int32, end.shape, 0) < rows[0]
    sol[...] = jnp.where(live, end, 0.0).astype(BF)
    each = fwd.shape[0] // 4
    diff = fwd[...].astype(F32)
    for who, ref in pieces(x, (w0, w1, w2, w3)):
        count = ref.shape[0] - each
        diff = diff - mul_t(ref[each:], sol[pl.ds(pl.multiple_of(who * count, count), count)])
    fwd_ref = back
    fwd_ref[...] = diff.astype(BF)
    total = None
    for who, ref in pieces(x, (w0, w1, w2, w3)):
        term = mul_t(ref[:each], fwd_ref[pl.ds(pl.multiple_of(who * each, each), each)])
        total = term if total is None else total + term
    back[...] = total.astype(BF)


def fold_kernel(at, pack, came, coup, came_coup, leaf_coup, fwd_leaf, leaf_inv, fold_t, inv_t, rest, full, fold):
    high = at[0] % 2
    half, sep = coup.shape
    width = came_coup.shape[1]
    mine_at = pl.multiple_of(high * half, half)
    other_at = pl.multiple_of((1 - high) * half, half)
    mine = mul(pack[:, :sep], leaf_coup[...]).astype(BF)
    other = mul(came[:, :sep], leaf_coup[...]).astype(BF)
    full[pl.ds(mine_at, half)] = mine
    full[pl.ds(other_at, half)] = other
    rest[...] = (
        fwd_leaf[...].astype(F32)
        - mul_t(mine, pack[:, sep + sep - width :])
        - mul_t(other, came[:, sep + sep - width :])
    )
    fold[pl.ds(mine_at, half)] = mul(coup[...], full[...]).astype(BF)
    win = pl.multiple_of(high * (sep - width), LANES)
    out = pl.multiple_of((1 - high) * width, LANES)
    fold[pl.ds(other_at, half)] = (
        mul(came_coup[...], full[pl.ds(win, width)])
        + mul(came[:, sep : sep + sep - width], full[pl.ds(out, sep - width)])
    ).astype(BF)
    fold_t[...] = fold[...].T
    inv_t[...] = leaf_inv[...].T


def last_kernel(at, fold_t, inv_t, rest, own, near, nxt, far, out, back):
    share = own.shape[1]
    for who, ref in pieces(at[0], (own, near, nxt, far)):
        back[:, pl.ds(pl.multiple_of(who * share, LANES), share)] = ref[...]
    diff = (rest[...] + mul(fold_t[...], back[...])).astype(BF)
    out[...] = mul(inv_t[...], diff).astype(BF)


def per_device(
    port_loads,
    leaf_inverse,
    leaf_coupling,
    first_inverse,
    second_coupling,
    second_inverse,
    border_coupling,
    border_inverse,
    border_rows,
):
    x = lax.axis_index("x")
    at = x.astype(jnp.int32)[None]
    low = x % 2 == 0
    group = lax.axis_size(GROUP)
    loads, leaf_inv, leaf_coup = port_loads[0, 0], leaf_inverse[0, 0], leaf_coupling[0, 0]
    inv_one, coup_two = first_inverse[0], second_coupling[0]
    half, sep = inv_one.shape
    leaf, ports = loads.shape
    share = ports // 4
    width = -(-half // LANES) * LANES
    border = border_inverse.shape[0]

    window = jnp.where(low, coup_two[:, sep - width :], coup_two[:, :width])
    block = jnp.concatenate([second_inverse[0], border_coupling[0]], 0)
    w_near = send(block, NEAR)
    came_coup = send(window, NEAR)
    w_next = send(block, NEXT)
    fwd_leaf, top, bot = call(
        leaf_kernel,
        [((leaf, ports), BF), ((half, ports), BF), ((half, ports), BF)],
        [],
        loads,
        leaf_inv,
        leaf_coup,
        flops=2 * leaf * ports * (leaf + sep),
    )
    came_top = send(top, NEAR)
    came_bot = send(bot, DOWN)
    w_far = send(w_near, NEXT)
    quarter = ((sep, share), BF)
    pack, own, near, nxt, far = call(
        first_kernel,
        [((half, 2 * sep - width + ports), BF)] + [quarter] * 4,
        [((sep, ports), BF), ((width, ports), BF), ((width, ports), BF)],
        at,
        inv_one,
        top,
        bot,
        came_top,
        came_bot,
        coup_two,
        came_coup,
        flops=2 * half * ports * sep + 2 * sep * ports * width,
    )
    far = send(far, ACROSS)
    nxt = send(nxt, NEXT)
    near = send(near, NEAR)
    late_pack, near = lax.optimization_barrier((pack, near))
    came_pack = send(late_pack, NEAR)
    blocks = (block, w_near, w_next, w_far)
    fwd_two, tiles = call(
        second_kernel,
        [quarter, ((border, share), BF)],
        [quarter],
        at,
        border_rows,
        own,
        near,
        nxt,
        far,
        *blocks,
        flops=2 * sep * share * (sep + border),
    )
    tiles = tiles.reshape(group, border // group, share)
    share_sum = jnp.sum(to_group(tiles).astype(F32), axis=0)
    rhs_share = (-share_sum).astype(BF)
    rhs_border = to_group(jnp.broadcast_to(rhs_share, tiles.shape)).reshape(border, share)
    (back_two,) = call(
        border_kernel,
        [quarter],
        [((border, share), BF)],
        at,
        border_rows,
        rhs_border,
        border_inverse,
        fwd_two,
        *blocks,
        flops=2 * share * (2 * border * border + border * sep + sep * sep),
    )
    back_far = send(back_two, ACROSS)
    back_next = send(back_two, NEXT)
    back_near = send(back_two, NEAR)
    pack, came_pack, back_two = lax.optimization_barrier((pack, came_pack, back_two))
    fold_t, inv_t, rest = call(
        fold_kernel,
        [((leaf, sep), BF), ((leaf, leaf), BF), ((leaf, ports), F32)],
        [((sep, leaf), BF), ((sep, leaf), BF)],
        at,
        pack,
        came_pack,
        coup_two,
        came_coup,
        leaf_coup,
        fwd_leaf,
        leaf_inv,
        flops=2 * sep * leaf * (2 * sep + ports),
    )
    (out,) = call(
        last_kernel,
        [((leaf, ports), BF)],
        [((sep, ports), BF)],
        at,
        fold_t,
        inv_t,
        rest,
        back_two,
        back_near,
        back_next,
        back_far,
        flops=2 * leaf * ports * (sep + leaf),
    )
    return out[None, None]


def solution(mesh):
    split = Mesh(mesh.devices.reshape(4, 4, 8, 2, 2), AXES)
    reg, sub = ("y", "zh", "c"), ("zl", "x")
    return jax.shard_map(
        per_device,
        mesh=split,
        in_specs=(P(reg, sub),) * 7 + (P(None, None), P(reg)),
        out_specs=P(reg, sub),
        check_vma=False,
    )
```

```python
import jax
import jax.numpy as jnp
from jax import lax
from jax.experimental import pallas as pl
from jax.experimental.pallas import tpu as pltpu
from jax.sharding import Mesh
from jax.sharding import PartitionSpec as P


AXES = ("zl", "x", "y", "zh", "c")
GROUP = ("zl", "y", "zh", "c")
NEAR = [(0, 1), (1, 0), (2, 3), (3, 2)]
NEXT = [(0, 3), (3, 0), (1, 2), (2, 1)]
ACROSS = [(0, 2), (2, 0), (1, 3), (3, 1)]
DOWN = [(0, 1), (2, 3)]
UP = [(1, 0), (3, 2)]
BACK = [(0, 3), (2, 1)]
BF = jnp.bfloat16
F32 = jnp.float32

LANES = 128


def send(x, pairs):
    return lax.ppermute(x, "x", pairs)


def to_group(tiles):
    return lax.all_to_all(tiles, GROUP, split_axis=0, concat_axis=0, tiled=True)


def mul(a, b):
    return jnp.dot(a, b, preferred_element_type=F32)


def mul_t(a, b):
    return lax.dot_general(a, b, (((0,), (0,)), ((), ())), preferred_element_type=F32)


def call(kernel, outs, scratch, *args, flops=0):
    moved = sum(a.size * a.dtype.itemsize for a in args)
    space = pl.BlockSpec(memory_space=pltpu.VMEM)
    return pl.pallas_call(
        kernel,
        out_shape=[jax.ShapeDtypeStruct(s, d) for s, d in outs],
        in_specs=[
            pl.BlockSpec(memory_space=pltpu.SMEM) if a.dtype == jnp.int32 else space
            for a in args
        ],
        out_specs=[space] * len(outs),
        scratch_shapes=[pltpu.VMEM(s, d) for s, d in scratch],
        compiler_params=pltpu.CompilerParams(vmem_limit_bytes=24 << 20),
        cost_estimate=pl.CostEstimate(flops=flops, bytes_accessed=moved, transcendentals=0),
    )(*args)


def others(x):
    return x ^ 1, 3 - x, x ^ 2


def leaf_kernel(loads, inv, coup, fwd, top, bot):
    fwd[...] = mul(inv[...], loads[...]).astype(BF)
    half = top.shape[0]
    top[...] = mul(coup[:half], fwd[...]).astype(BF)
    bot[...] = mul(coup[half:], fwd[...]).astype(BF)


def first_kernel(at, inv, top, bot, came_top, came_bot, coup, came_coup, pack, own, near, nxt, far, rhs, held, turned):
    x = at[0]
    high = x % 2
    half, sep = inv.shape
    ports = top.shape[1]
    width = held.shape[0]
    rhs[:half] = (-(top[...].astype(F32) + came_top[...].astype(F32))).astype(BF)
    rhs[half:] = (-(bot[...].astype(F32) + came_bot[...].astype(F32))).astype(BF)
    fwd = mul(inv[...], rhs[...]).astype(BF)
    pack[:, :sep] = inv[...]
    pack[:, sep + sep - width :] = fwd
    pad = width - half
    held[:pad] = jnp.zeros((pad, ports), BF)
    held[half:] = jnp.zeros((pad, ports), BF)
    start = pl.multiple_of(high * pad, pad)
    held[pl.ds(start, half)] = fwd
    lane = pl.multiple_of(high * (sep - width), LANES)
    rest = pl.multiple_of(high * width, LANES)
    pack[:, sep : sep + sep - width] = coup[:, pl.ds(rest, sep - width)]
    mine = coup[:, pl.ds(lane, width)]
    mine_at = pl.multiple_of(high * half, half)
    other_at = pl.multiple_of((1 - high) * half, half)
    share = own.shape[1]
    for at_col, who in enumerate((x,) + others(x)):
        cols = pl.ds(pl.multiple_of(who * share, LANES), share)
        turned[:, at_col * share : (at_col + 1) * share] = held[:, cols]
    for weights, row in ((mine, mine_at), (came_coup[...], other_at)):
        part = mul(weights, turned[...]).astype(BF)
        for at_col, ref in enumerate((own, near, nxt, far)):
            ref[pl.ds(row, half)] = part[:, at_col * share : (at_col + 1) * share]


def pieces(x, refs):
    return zip((x,) + others(x), refs)


def join_kernel(at, i0, i1, i2, i3, b0, up, nxt, down, border_inv, inv, inv_t, coup, coup_t, border_t):
    x = at[0]
    each = i0.shape[0]
    for who, ref in pieces(x, (i0, i1, i2, i3)):
        inv[pl.ds(pl.multiple_of(who * each, each), each)] = ref[...]
    count = b0.shape[0]
    near = up[:count] + down[count:]
    far = up[count:] + down[:count]
    for who, block in pieces(x, (b0[...], near, nxt[...], far)):
        coup[pl.ds(pl.multiple_of(who * count, count), count)] = block
    inv_t[...] = inv[...].T
    coup_t[...] = coup[...].T
    border_t[...] = border_inv[...].T


def second_kernel(rows, own, near, nxt, far, inv, coup, fwd, tiles):
    total = own[...].astype(F32) + near[...].astype(F32)
    total = total + (nxt[...].astype(F32) + far[...].astype(F32))
    fwd[...] = mul(inv[...], (-total).astype(BF)).astype(BF)
    part = mul(coup[...], fwd[...])
    live = lax.broadcasted_iota(jnp.int32, part.shape, 0) < rows[0]
    tiles[...] = jnp.where(live, part, 0.0).astype(BF)


def border_kernel(rows, rhs, inv, inv_t, fwd, second_t, coup_t, back):
    mid = mul(inv[...], rhs[...]).astype(BF)
    end = mul(inv_t[...], mid)
    live = lax.broadcasted_iota(jnp.int32, end.shape, 0) < rows[0]
    sol = jnp.where(live, end, 0.0).astype(BF)
    diff = (fwd[...].astype(F32) - mul(coup_t[...], sol)).astype(BF)
    back[...] = mul(second_t[...], diff).astype(BF)


def fold_kernel(at, pack, came, coup, came_coup, leaf_coup, fwd_leaf, leaf_inv, fold_t, inv_t, rest, full, fold):
    high = at[0] % 2
    half, sep = coup.shape
    width = came_coup.shape[1]
    mine_at = pl.multiple_of(high * half, half)
    other_at = pl.multiple_of((1 - high) * half, half)
    mine = mul(pack[:, :sep], leaf_coup[...]).astype(BF)
    other = mul(came[:, :sep], leaf_coup[...]).astype(BF)
    full[pl.ds(mine_at, half)] = mine
    full[pl.ds(other_at, half)] = other
    rest[...] = (
        fwd_leaf[...].astype(F32)
        - mul_t(mine, pack[:, sep + sep - width :])
        - mul_t(other, came[:, sep + sep - width :])
    )
    fold[pl.ds(mine_at, half)] = mul(coup[...], full[...]).astype(BF)
    win = pl.multiple_of(high * (sep - width), LANES)
    out = pl.multiple_of((1 - high) * width, LANES)
    fold[pl.ds(other_at, half)] = (
        mul(came_coup[...], full[pl.ds(win, width)])
        + mul(came[:, sep : sep + sep - width], full[pl.ds(out, sep - width)])
    ).astype(BF)
    fold_t[...] = fold[...].T
    inv_t[...] = leaf_inv[...].T


def last_kernel(at, fold_t, inv_t, rest, own, near, nxt, far, out, back):
    share = own.shape[1]
    for who, ref in pieces(at[0], (own, near, nxt, far)):
        back[:, pl.ds(pl.multiple_of(who * share, LANES), share)] = ref[...]
    diff = (rest[...] + mul(fold_t[...], back[...])).astype(BF)
    out[...] = mul(inv_t[...], diff).astype(BF)


def per_device(
    port_loads,
    leaf_inverse,
    leaf_coupling,
    first_inverse,
    second_coupling,
    second_inverse,
    border_coupling,
    border_inverse,
    border_rows,
):
    x = lax.axis_index("x")
    at = x.astype(jnp.int32)[None]
    low = x % 2 == 0
    group = lax.axis_size(GROUP)
    loads, leaf_inv, leaf_coup = port_loads[0, 0], leaf_inverse[0, 0], leaf_coupling[0, 0]
    inv_one, coup_two = first_inverse[0], second_coupling[0]
    half, sep = inv_one.shape
    leaf, ports = loads.shape
    share = ports // 4
    width = -(-half // LANES) * LANES
    border = border_inverse.shape[0]

    inv_two, coup_border = second_inverse[0], border_coupling[0]
    i_near = send(inv_two, NEAR)
    b_next = send(coup_border, NEXT)
    fwd_leaf, top, bot = call(
        leaf_kernel,
        [((leaf, ports), BF), ((half, ports), BF), ((half, ports), BF)],
        [],
        loads,
        leaf_inv,
        leaf_coup,
        flops=2 * leaf * ports * (leaf + sep),
    )
    came_bot = send(bot, DOWN)
    b_up = send(jnp.concatenate([coup_border, b_next], 0), UP)
    window = jnp.where(low, coup_two[:, sep - width :], coup_two[:, :width])
    came_coup = send(window, NEAR)
    came_top = send(top, NEAR)
    i_next = send(inv_two, NEXT)
    i_far = send(i_near, NEXT)
    b_down = send(b_up, BACK)
    quarter = ((sep, share), BF)
    pack, own, near, nxt, far = call(
        first_kernel,
        [((half, 2 * sep - width + ports), BF)] + [quarter] * 4,
        [((sep, ports), BF), ((width, ports), BF), ((width, ports), BF)],
        at,
        inv_one,
        top,
        bot,
        came_top,
        came_bot,
        coup_two,
        came_coup,
        flops=2 * half * ports * sep + 2 * sep * ports * width,
    )
    near = send(near, NEAR)
    far = send(far, ACROSS)
    nxt = send(nxt, NEXT)
    late_pack, near = lax.optimization_barrier((pack, near))
    came_pack = send(late_pack, NEAR)
    inv_full, inv_full_t, coup_full, coup_full_t, border_t = call(
        join_kernel,
        [
            ((sep, sep), BF),
            ((sep, sep), BF),
            ((border, sep), BF),
            ((sep, border), BF),
            ((border, border), BF),
        ],
        [],
        at,
        inv_two,
        i_near,
        i_next,
        i_far,
        coup_border,
        b_up,
        b_next,
        b_down,
        border_inverse,
    )
    fwd_two, tiles = call(
        second_kernel,
        [quarter, ((border, share), BF)],
        [],
        border_rows,
        own,
        near,
        nxt,
        far,
        inv_full,
        coup_full,
        flops=2 * sep * share * (sep + border),
    )
    tiles = tiles.reshape(group, border // group, share)
    share_sum = jnp.sum(to_group(tiles).astype(F32), axis=0)
    rhs_share = (-share_sum).astype(BF)
    rhs_border = to_group(jnp.broadcast_to(rhs_share, tiles.shape)).reshape(border, share)
    (back_two,) = call(
        border_kernel,
        [quarter],
        [],
        border_rows,
        rhs_border,
        border_inverse,
        border_t,
        fwd_two,
        inv_full_t,
        coup_full_t,
        flops=2 * share * (2 * border * border + border * sep + sep * sep),
    )
    back_far = send(back_two, ACROSS)
    back_next = send(back_two, NEXT)
    back_near = send(back_two, NEAR)
    pack, came_pack, back_two = lax.optimization_barrier((pack, came_pack, back_two))
    fold_t, inv_t, rest = call(
        fold_kernel,
        [((leaf, sep), BF), ((leaf, leaf), BF), ((leaf, ports), F32)],
        [((sep, leaf), BF), ((sep, leaf), BF)],
        at,
        pack,
        came_pack,
        coup_two,
        came_coup,
        leaf_coup,
        fwd_leaf,
        leaf_inv,
        flops=2 * sep * leaf * (2 * sep + ports),
    )
    (out,) = call(
        last_kernel,
        [((leaf, ports), BF)],
        [((sep, ports), BF)],
        at,
        fold_t,
        inv_t,
        rest,
        back_two,
        back_near,
        back_next,
        back_far,
        flops=2 * leaf * ports * (sep + leaf),
    )
    return out[None, None]


def solution(mesh):
    split = Mesh(mesh.devices.reshape(4, 4, 8, 2, 2), AXES)
    reg, sub = ("y", "zh", "c"), ("zl", "x")
    return jax.shard_map(
        per_device,
        mesh=split,
        in_specs=(P(reg, sub),) * 7 + (P(None, None), P(reg)),
        out_specs=P(reg, sub),
        check_vma=False,
    )
```

```python
import jax
import jax.numpy as jnp
from jax import lax
from jax.experimental import pallas as pl
from jax.experimental.pallas import tpu as pltpu
from jax.sharding import Mesh
from jax.sharding import PartitionSpec as P


AXES = ("zl", "x", "y", "zh", "c")
GROUP = ("zl", "y", "zh", "c")
NEAR = [(0, 1), (1, 0), (2, 3), (3, 2)]
NEXT = [(0, 3), (3, 0), (1, 2), (2, 1)]
ACROSS = [(0, 2), (2, 0), (1, 3), (3, 1)]
DOWN = [(0, 1), (2, 3)]
UP = [(1, 0), (3, 2)]
BACK = [(0, 3), (2, 1)]
BF = jnp.bfloat16
F32 = jnp.float32

LANES = 128


def send(x, pairs):
    return lax.ppermute(x, "x", pairs)


def to_group(tiles):
    return lax.all_to_all(tiles, GROUP, split_axis=0, concat_axis=0, tiled=True)


def mul(a, b):
    return jnp.dot(a, b, preferred_element_type=F32)


def mul_t(a, b):
    return lax.dot_general(a, b, (((0,), (0,)), ((), ())), preferred_element_type=F32)


def call(kernel, outs, scratch, *args, flops=0):
    moved = sum(a.size * a.dtype.itemsize for a in args)
    space = pl.BlockSpec(memory_space=pltpu.VMEM)
    return pl.pallas_call(
        kernel,
        out_shape=[jax.ShapeDtypeStruct(s, d) for s, d in outs],
        in_specs=[
            pl.BlockSpec(memory_space=pltpu.SMEM) if a.dtype == jnp.int32 else space
            for a in args
        ],
        out_specs=[space] * len(outs),
        scratch_shapes=[pltpu.VMEM(s, d) for s, d in scratch],
        compiler_params=pltpu.CompilerParams(vmem_limit_bytes=16 << 20),
        cost_estimate=pl.CostEstimate(flops=flops, bytes_accessed=moved, transcendentals=0),
    )(*args)


def others(x):
    return x ^ 1, 3 - x, x ^ 2


def leaf_kernel(loads_hbm, inv_hbm, coup_hbm, top, bot, loads, inv, coup, sems):
    copies = [
        pltpu.make_async_copy(src, dst, sems.at[n])
        for n, (src, dst) in enumerate(
            ((loads_hbm, loads), (inv_hbm, inv), (coup_hbm, coup))
        )
    ]
    for copy in copies:
        copy.start()
    copies[0].wait()
    copies[1].wait()
    fwd = mul(inv[...], loads[...]).astype(BF)
    copies[2].wait()
    half = top.shape[0]
    bot[...] = mul(coup[half:], fwd).astype(BF)
    top[...] = mul(coup[:half], fwd).astype(BF)


def leaf_call(loads, inv, coup, half):
    args = [pltpu.with_memory_space_constraint(a, pltpu.HBM) for a in (loads, inv, coup)]
    ports = loads.shape[1]
    shape = jax.ShapeDtypeStruct((half, ports), BF)
    return pl.pallas_call(
        leaf_kernel,
        name="k_leaf",
        out_shape=[shape, shape],
        in_specs=[pl.BlockSpec(memory_space=pltpu.HBM)] * 3,
        out_specs=[pl.BlockSpec(memory_space=pltpu.VMEM)] * 2,
        scratch_shapes=[pltpu.VMEM(a.shape, a.dtype) for a in (loads, inv, coup)]
        + [pltpu.SemaphoreType.DMA((3,))],
        compiler_params=pltpu.CompilerParams(vmem_limit_bytes=8 << 20),
    )(*args)


def first_kernel(at, inv, top, bot, came_top, came_bot, coup, came_coup, pack, own, near, nxt, far, rhs, held, turned):
    x = at[0]
    high = x % 2
    half, sep = inv.shape
    ports = top.shape[1]
    width = held.shape[0]
    rhs[:half] = (-(top[...].astype(F32) + came_top[...].astype(F32))).astype(BF)
    rhs[half:] = (-(bot[...].astype(F32) + came_bot[...].astype(F32))).astype(BF)
    fwd = mul(inv[...], rhs[...]).astype(BF)
    pack[:, :sep] = inv[...]
    pack[:, sep + sep - width :] = fwd
    pad = width - half
    held[:pad] = jnp.zeros((pad, ports), BF)
    held[half:] = jnp.zeros((pad, ports), BF)
    start = pl.multiple_of(high * pad, pad)
    held[pl.ds(start, half)] = fwd
    lane = pl.multiple_of(high * (sep - width), LANES)
    rest = pl.multiple_of(high * width, LANES)
    pack[:, sep : sep + sep - width] = coup[:, pl.ds(rest, sep - width)]
    mine = coup[:, pl.ds(lane, width)]
    mine_at = pl.multiple_of(high * half, half)
    other_at = pl.multiple_of((1 - high) * half, half)
    share = own.shape[1]
    for at_col, who in enumerate((x,) + others(x)):
        cols = pl.ds(pl.multiple_of(who * share, LANES), share)
        turned[:, at_col * share : (at_col + 1) * share] = held[:, cols]
    for weights, row in ((mine, mine_at), (came_coup[...], other_at)):
        part = mul(weights, turned[...]).astype(BF)
        for at_col, ref in enumerate((own, near, nxt, far)):
            ref[pl.ds(row, half)] = part[:, at_col * share : (at_col + 1) * share]


def pieces(x, refs):
    return zip((x,) + others(x), refs)


def join_kernel(at, i0, i1, i2, i3, b0, up, nxt, down, inv, coup):
    x = at[0]
    each = i0.shape[0]
    for who, ref in pieces(x, (i0, i1, i2, i3)):
        inv[pl.ds(pl.multiple_of(who * each, each), each)] = ref[...]
    count = b0.shape[0]
    near = up[:count] + down[count:]
    far = up[count:] + down[:count]
    for who, block in pieces(x, (b0[...], near, nxt[...], far)):
        coup[pl.ds(pl.multiple_of(who * count, count), count)] = block


def second_kernel(rows, own, near, nxt, far, inv, coup, fwd, tiles):
    total = own[...].astype(F32) + near[...].astype(F32)
    total = total + (nxt[...].astype(F32) + far[...].astype(F32))
    fwd[...] = mul(inv[...], (-total).astype(BF)).astype(BF)
    part = mul(coup[...], fwd[...])
    live = lax.broadcasted_iota(jnp.int32, part.shape, 0) < rows[0]
    tiles[...] = jnp.where(live, part, 0.0).astype(BF)


def border_kernel(rows, rhs, inv, fwd, second, coup, back):
    mid = mul(inv[...], rhs[...]).astype(BF)
    end = mul_t(inv[...], mid)
    live = lax.broadcasted_iota(jnp.int32, end.shape, 0) < rows[0]
    sol = jnp.where(live, end, 0.0).astype(BF)
    diff = (fwd[...].astype(F32) - mul_t(coup[...], sol)).astype(BF)
    back[...] = mul_t(second[...], diff).astype(BF)


def fold_kernel(at, pack, came, coup, came_coup, leaf_coup, loads, leaf_inv, fold_t, inv_t, rest, full, fold):
    high = at[0] % 2
    half, sep = coup.shape
    width = came_coup.shape[1]
    mine_at = pl.multiple_of(high * half, half)
    other_at = pl.multiple_of((1 - high) * half, half)
    mine = mul(pack[:, :sep], leaf_coup[...]).astype(BF)
    other = mul(came[:, :sep], leaf_coup[...]).astype(BF)
    full[pl.ds(mine_at, half)] = mine
    full[pl.ds(other_at, half)] = other
    rest[...] = (
        mul(leaf_inv[...], loads[...]).astype(BF).astype(F32)
        - mul_t(mine, pack[:, sep + sep - width :])
        - mul_t(other, came[:, sep + sep - width :])
    )
    fold[pl.ds(mine_at, half)] = mul(coup[...], full[...]).astype(BF)
    win = pl.multiple_of(high * (sep - width), LANES)
    out = pl.multiple_of((1 - high) * width, LANES)
    fold[pl.ds(other_at, half)] = (
        mul(came_coup[...], full[pl.ds(win, width)])
        + mul(came[:, sep : sep + sep - width], full[pl.ds(out, sep - width)])
    ).astype(BF)
    fold_t[...] = fold[...].T
    inv_t[...] = leaf_inv[...].T


def last_kernel(at, fold_t, inv_t, rest, own, near, nxt, far, out, back):
    share = own.shape[1]
    for who, ref in pieces(at[0], (own, near, nxt, far)):
        back[:, pl.ds(pl.multiple_of(who * share, LANES), share)] = ref[...]
    diff = (rest[...] + mul(fold_t[...], back[...])).astype(BF)
    out[...] = mul(inv_t[...], diff).astype(BF)


def per_device(
    port_loads,
    leaf_inverse,
    leaf_coupling,
    first_inverse,
    second_coupling,
    second_inverse,
    border_coupling,
    border_inverse,
    border_rows,
):
    x = lax.axis_index("x")
    at = x.astype(jnp.int32)[None]
    low = x % 2 == 0
    group = lax.axis_size(GROUP)
    loads, leaf_inv, leaf_coup = port_loads[0, 0], leaf_inverse[0, 0], leaf_coupling[0, 0]
    inv_one, coup_two = first_inverse[0], second_coupling[0]
    half, sep = inv_one.shape
    leaf, ports = loads.shape
    share = ports // 4
    width = -(-half // LANES) * LANES
    border = border_inverse.shape[0]

    inv_two, coup_border = second_inverse[0], border_coupling[0]
    i_near = send(inv_two, NEAR)
    b_next = send(coup_border, NEXT)
    top, bot = leaf_call(loads, leaf_inv, leaf_coup, half)
    came_bot = send(bot, DOWN)
    b_up = send(jnp.concatenate([coup_border, b_next], 0), UP)
    window = jnp.where(low, coup_two[:, sep - width :], coup_two[:, :width])
    came_coup = send(window, NEAR)
    came_top = send(top, NEAR)
    i_next = send(inv_two, NEXT)
    i_far = send(i_near, NEXT)
    b_down = send(b_up, BACK)
    quarter = ((sep, share), BF)
    pack, own, near, nxt, far = call(
        first_kernel,
        [((half, 2 * sep - width + ports), BF)] + [quarter] * 4,
        [((sep, ports), BF), ((width, ports), BF), ((width, ports), BF)],
        at,
        inv_one,
        top,
        bot,
        came_top,
        came_bot,
        coup_two,
        came_coup,
        flops=2 * half * ports * sep + 2 * sep * ports * width,
    )
    near = send(near, NEAR)
    far = send(far, ACROSS)
    nxt = send(nxt, NEXT)
    late_pack, near = lax.optimization_barrier((pack, near))
    came_pack = send(late_pack, NEAR)
    inv_full, coup_full = call(
        join_kernel,
        [((sep, sep), BF), ((border, sep), BF)],
        [],
        at,
        inv_two,
        i_near,
        i_next,
        i_far,
        coup_border,
        b_up,
        b_next,
        b_down,
    )
    fwd_two, tiles = call(
        second_kernel,
        [quarter, ((border, share), BF)],
        [],
        border_rows,
        own,
        near,
        nxt,
        far,
        inv_full,
        coup_full,
        flops=2 * sep * share * (sep + border),
    )
    tiles = tiles.reshape(group, border // group, share)
    share_sum = jnp.sum(to_group(tiles).astype(F32), axis=0)
    rhs_share = (-share_sum).astype(BF)
    rhs_border = to_group(jnp.broadcast_to(rhs_share, tiles.shape)).reshape(border, share)
    (back_two,) = call(
        border_kernel,
        [quarter],
        [],
        border_rows,
        rhs_border,
        border_inverse,
        fwd_two,
        inv_full,
        coup_full,
        flops=2 * share * (2 * border * border + border * sep + sep * sep),
    )
    back_far = send(back_two, ACROSS)
    back_next = send(back_two, NEXT)
    back_near = send(back_two, NEAR)
    pack, came_pack, back_two = lax.optimization_barrier((pack, came_pack, back_two))
    fold_t, inv_t, rest = call(
        fold_kernel,
        [((leaf, sep), BF), ((leaf, leaf), BF), ((leaf, ports), F32)],
        [((sep, leaf), BF), ((sep, leaf), BF)],
        at,
        pack,
        came_pack,
        coup_two,
        came_coup,
        leaf_coup,
        loads,
        leaf_inv,
        flops=2 * sep * leaf * (2 * sep + ports),
    )
    (out,) = call(
        last_kernel,
        [((leaf, ports), BF)],
        [((sep, ports), BF)],
        at,
        fold_t,
        inv_t,
        rest,
        back_two,
        back_near,
        back_next,
        back_far,
        flops=2 * leaf * ports * (sep + leaf),
    )
    return out[None, None]


def solution(mesh):
    split = Mesh(mesh.devices.reshape(4, 4, 8, 2, 2), AXES)
    reg, sub = ("y", "zh", "c"), ("zl", "x")
    return jax.shard_map(
        per_device,
        mesh=split,
        in_specs=(P(reg, sub),) * 7 + (P(None, None), P(reg)),
        out_specs=P(reg, sub),
        check_vma=False,
    )
```

```python
import jax
import jax.numpy as jnp
from jax import lax
from jax.experimental import pallas as pl
from jax.experimental.pallas import tpu as pltpu
from jax.sharding import Mesh
from jax.sharding import PartitionSpec as P


AXES = ("zl", "x", "y", "zh", "c")
GROUP = ("zl", "y", "zh", "c")
NEAR = [(0, 1), (1, 0), (2, 3), (3, 2)]
NEXT = [(0, 3), (3, 0), (1, 2), (2, 1)]
ACROSS = [(0, 2), (2, 0), (1, 3), (3, 1)]
DOWN = [(0, 1), (2, 3)]
UP = [(1, 0), (3, 2)]
BACK = [(0, 3), (2, 1)]
BF = jnp.bfloat16
F32 = jnp.float32

LANES = 128
CHUNK = 256


def send(x, pairs):
    return lax.ppermute(x, "x", pairs)


def to_group(tiles):
    return lax.all_to_all(tiles, GROUP, split_axis=0, concat_axis=0, tiled=True)


def mul(a, b):
    return jnp.dot(a, b, preferred_element_type=F32)


def mul_t(a, b):
    return lax.dot_general(a, b, (((0,), (0,)), ((), ())), preferred_element_type=F32)


def call(kernel, outs, scratch, *args, flops=0):
    moved = sum(a.size * a.dtype.itemsize for a in args)
    space = pl.BlockSpec(memory_space=pltpu.VMEM)
    return pl.pallas_call(
        kernel,
        out_shape=[jax.ShapeDtypeStruct(s, d) for s, d in outs],
        in_specs=[
            pl.BlockSpec(memory_space=pltpu.SMEM) if a.dtype == jnp.int32 else space
            for a in args
        ],
        out_specs=[space] * len(outs),
        scratch_shapes=[pltpu.VMEM(s, d) for s, d in scratch],
        compiler_params=pltpu.CompilerParams(vmem_limit_bytes=16 << 20),
        cost_estimate=pl.CostEstimate(flops=flops, bytes_accessed=moved, transcendentals=0),
    )(*args)


def lower_mul(lower, vector, out):
    size = vector.shape[0]
    for first in range(0, size, CHUNK):
        last = min(first + CHUNK, size)
        out[first:last] = mul(lower[first:last, :last], vector[:last]).astype(out.dtype)


def lower_mul_t(lower, vector, out):
    size = vector.shape[0]
    for first in range(0, size, CHUNK):
        last = min(first + CHUNK, size)
        out[first:last] = mul_t(lower[first:, first:last], vector[first:]).astype(out.dtype)


def others(x):
    return x ^ 1, 3 - x, x ^ 2


def leaf_kernel(loads_hbm, inv_hbm, coup_hbm, top, bot, loads, inv, coup, sems):
    copies = [
        pltpu.make_async_copy(src, dst, sems.at[n])
        for n, (src, dst) in enumerate(
            ((loads_hbm, loads), (inv_hbm, inv), (coup_hbm, coup))
        )
    ]
    for copy in copies:
        copy.start()
    copies[0].wait()
    copies[1].wait()
    fwd = mul(inv[...], loads[...]).astype(BF)
    copies[2].wait()
    half = top.shape[0]
    bot[...] = mul(coup[half:], fwd).astype(BF)
    top[...] = mul(coup[:half], fwd).astype(BF)


def leaf_call(loads, inv, coup, half):
    args = [pltpu.with_memory_space_constraint(a, pltpu.HBM) for a in (loads, inv, coup)]
    ports = loads.shape[1]
    shape = jax.ShapeDtypeStruct((half, ports), BF)
    return pl.pallas_call(
        leaf_kernel,
        name="k_leaf",
        out_shape=[shape, shape],
        in_specs=[pl.BlockSpec(memory_space=pltpu.HBM)] * 3,
        out_specs=[pl.BlockSpec(memory_space=pltpu.VMEM)] * 2,
        scratch_shapes=[pltpu.VMEM(a.shape, a.dtype) for a in (loads, inv, coup)]
        + [pltpu.SemaphoreType.DMA((3,))],
        compiler_params=pltpu.CompilerParams(vmem_limit_bytes=8 << 20),
    )(*args)


def first_kernel(at, inv, top, bot, came_top, came_bot, coup, came_coup, pack, own, near, nxt, far, rhs, held, turned):
    x = at[0]
    high = x % 2
    half, sep = inv.shape
    ports = top.shape[1]
    width = held.shape[0]
    rhs[:half] = (-(top[...].astype(F32) + came_top[...].astype(F32))).astype(BF)
    rhs[half:] = (-(bot[...].astype(F32) + came_bot[...].astype(F32))).astype(BF)
    fwd = mul(inv[...], rhs[...]).astype(BF)
    pack[:, :sep] = inv[...]
    pack[:, sep + sep - width :] = fwd
    pad = width - half
    held[:pad] = jnp.zeros((pad, ports), BF)
    held[half:] = jnp.zeros((pad, ports), BF)
    start = pl.multiple_of(high * pad, pad)
    held[pl.ds(start, half)] = fwd
    lane = pl.multiple_of(high * (sep - width), LANES)
    rest = pl.multiple_of(high * width, LANES)
    pack[:, sep : sep + sep - width] = coup[:, pl.ds(rest, sep - width)]
    mine = coup[:, pl.ds(lane, width)]
    mine_at = pl.multiple_of(high * half, half)
    other_at = pl.multiple_of((1 - high) * half, half)
    share = own.shape[1]
    for at_col, who in enumerate((x,) + others(x)):
        cols = pl.ds(pl.multiple_of(who * share, LANES), share)
        turned[:, at_col * share : (at_col + 1) * share] = held[:, cols]
    for weights, row in ((mine, mine_at), (came_coup[...], other_at)):
        part = mul(weights, turned[...]).astype(BF)
        for at_col, ref in enumerate((own, near, nxt, far)):
            ref[pl.ds(row, half)] = part[:, at_col * share : (at_col + 1) * share]


def pieces(x, refs):
    return zip((x,) + others(x), refs)


def join_kernel(at, i0, i1, i2, i3, b0, up, nxt, down, inv, coup):
    x = at[0]
    each = i0.shape[0]
    for who, ref in pieces(x, (i0, i1, i2, i3)):
        inv[pl.ds(pl.multiple_of(who * each, each), each)] = ref[...]
    count = b0.shape[0]
    near = up[:count] + down[count:]
    far = up[count:] + down[:count]
    for who, block in pieces(x, (b0[...], near, nxt[...], far)):
        coup[pl.ds(pl.multiple_of(who * count, count), count)] = block


def second_kernel(rows, own, near, nxt, far, inv, coup, fwd, tiles, rhs):
    total = own[...].astype(F32) + near[...].astype(F32)
    total = total + (nxt[...].astype(F32) + far[...].astype(F32))
    rhs[...] = (-total).astype(BF)
    lower_mul(inv, rhs, fwd)
    for first in range(0, tiles.shape[0], CHUNK):
        part = mul(coup[first : first + CHUNK], fwd[...])
        live = lax.broadcasted_iota(jnp.int32, part.shape, 0) + first < rows[0]
        tiles[first : first + CHUNK] = jnp.where(live, part, 0.0).astype(BF)


def border_kernel(rows, rhs, inv, fwd, second, coup, back, mid, sol, diff):
    lower_mul(inv, rhs, mid)
    lower_mul_t(inv, mid, sol)
    live = lax.broadcasted_iota(jnp.int32, sol.shape, 0) < rows[0]
    masked = jnp.where(live, sol[...], 0.0).astype(BF)
    diff[...] = (fwd[...].astype(F32) - mul_t(coup[...], masked)).astype(BF)
    lower_mul_t(second, diff, back)


def fold_kernel(at, pack, came, coup, came_coup, leaf_coup, loads, leaf_inv, fold_t, inv_t, rest, full, fold):
    high = at[0] % 2
    half, sep = coup.shape
    width = came_coup.shape[1]
    mine_at = pl.multiple_of(high * half, half)
    other_at = pl.multiple_of((1 - high) * half, half)
    mine = mul(pack[:, :sep], leaf_coup[...]).astype(BF)
    other = mul(came[:, :sep], leaf_coup[...]).astype(BF)
    full[pl.ds(mine_at, half)] = mine
    full[pl.ds(other_at, half)] = other
    rest[...] = (
        mul(leaf_inv[...], loads[...]).astype(BF).astype(F32)
        - mul_t(mine, pack[:, sep + sep - width :])
        - mul_t(other, came[:, sep + sep - width :])
    )
    fold[pl.ds(mine_at, half)] = mul(coup[...], full[...]).astype(BF)
    win = pl.multiple_of(high * (sep - width), LANES)
    out = pl.multiple_of((1 - high) * width, LANES)
    fold[pl.ds(other_at, half)] = (
        mul(came_coup[...], full[pl.ds(win, width)])
        + mul(came[:, sep : sep + sep - width], full[pl.ds(out, sep - width)])
    ).astype(BF)
    fold_t[...] = fold[...].T
    inv_t[...] = leaf_inv[...].T


def last_kernel(at, fold_t, inv_t, rest, own, near, nxt, far, out, back):
    share = own.shape[1]
    for who, ref in pieces(at[0], (own, near, nxt, far)):
        back[:, pl.ds(pl.multiple_of(who * share, LANES), share)] = ref[...]
    diff = (rest[...] + mul(fold_t[...], back[...])).astype(BF)
    out[...] = mul(inv_t[...], diff).astype(BF)


def per_device(
    port_loads,
    leaf_inverse,
    leaf_coupling,
    first_inverse,
    second_coupling,
    second_inverse,
    border_coupling,
    border_inverse,
    border_rows,
):
    x = lax.axis_index("x")
    at = x.astype(jnp.int32)[None]
    low = x % 2 == 0
    group = lax.axis_size(GROUP)
    loads, leaf_inv, leaf_coup = port_loads[0, 0], leaf_inverse[0, 0], leaf_coupling[0, 0]
    inv_one, coup_two = first_inverse[0], second_coupling[0]
    half, sep = inv_one.shape
    leaf, ports = loads.shape
    share = ports // 4
    width = -(-half // LANES) * LANES
    border = border_inverse.shape[0]

    inv_two, coup_border = second_inverse[0], border_coupling[0]
    i_near = send(inv_two, NEAR)
    b_next = send(coup_border, NEXT)
    top, bot = leaf_call(loads, leaf_inv, leaf_coup, half)
    came_bot = send(bot, DOWN)
    b_up = send(jnp.concatenate([coup_border, b_next], 0), UP)
    window = jnp.where(low, coup_two[:, sep - width :], coup_two[:, :width])
    came_coup = send(window, NEAR)
    came_top = send(top, NEAR)
    i_next = send(inv_two, NEXT)
    i_far = send(i_near, NEXT)
    b_down = send(b_up, BACK)
    quarter = ((sep, share), BF)
    pack, own, near, nxt, far = call(
        first_kernel,
        [((half, 2 * sep - width + ports), BF)] + [quarter] * 4,
        [((sep, ports), BF), ((width, ports), BF), ((width, ports), BF)],
        at,
        inv_one,
        top,
        bot,
        came_top,
        came_bot,
        coup_two,
        came_coup,
        flops=2 * half * ports * sep + 2 * sep * ports * width,
    )
    near = send(near, NEAR)
    far = send(far, ACROSS)
    nxt = send(nxt, NEXT)
    late_pack, near = lax.optimization_barrier((pack, near))
    came_pack = send(late_pack, NEAR)
    inv_full, coup_full = call(
        join_kernel,
        [((sep, sep), BF), ((border, sep), BF)],
        [],
        at,
        inv_two,
        i_near,
        i_next,
        i_far,
        coup_border,
        b_up,
        b_next,
        b_down,
    )
    fwd_two, tiles = call(
        second_kernel,
        [quarter, ((border, share), BF)],
        [quarter],
        border_rows,
        own,
        near,
        nxt,
        far,
        inv_full,
        coup_full,
        flops=2 * sep * share * (sep + border),
    )
    tiles = tiles.reshape(group, border // group, share)
    share_sum = jnp.sum(to_group(tiles).astype(F32), axis=0)
    rhs_share = (-share_sum).astype(BF)
    rhs_border = to_group(jnp.broadcast_to(rhs_share, tiles.shape)).reshape(border, share)
    (back_two,) = call(
        border_kernel,
        [quarter],
        [((border, share), BF), ((border, share), F32), quarter],
        border_rows,
        rhs_border,
        border_inverse,
        fwd_two,
        inv_full,
        coup_full,
        flops=2 * share * (2 * border * border + border * sep + sep * sep),
    )
    back_far = send(back_two, ACROSS)
    back_next = send(back_two, NEXT)
    back_near = send(back_two, NEAR)
    pack, came_pack, back_two = lax.optimization_barrier((pack, came_pack, back_two))
    fold_t, inv_t, rest = call(
        fold_kernel,
        [((leaf, sep), BF), ((leaf, leaf), BF), ((leaf, ports), F32)],
        [((sep, leaf), BF), ((sep, leaf), BF)],
        at,
        pack,
        came_pack,
        coup_two,
        came_coup,
        leaf_coup,
        loads,
        leaf_inv,
        flops=2 * sep * leaf * (2 * sep + ports),
    )
    (out,) = call(
        last_kernel,
        [((leaf, ports), BF)],
        [((sep, ports), BF)],
        at,
        fold_t,
        inv_t,
        rest,
        back_two,
        back_near,
        back_next,
        back_far,
        flops=2 * leaf * ports * (sep + leaf),
    )
    return out[None, None]


def solution(mesh):
    split = Mesh(mesh.devices.reshape(4, 4, 8, 2, 2), AXES)
    reg, sub = ("y", "zh", "c"), ("zl", "x")
    return jax.shard_map(
        per_device,
        mesh=split,
        in_specs=(P(reg, sub),) * 7 + (P(None, None), P(reg)),
        out_specs=P(reg, sub),
        check_vma=False,
    )
```

```python
import jax
import jax.numpy as jnp
from jax import lax
from jax.experimental import pallas as pl
from jax.experimental.pallas import tpu as pltpu
from jax.sharding import Mesh
from jax.sharding import PartitionSpec as P


AXES = ("zl", "x", "y", "zh", "c")
GROUP = ("zl", "y", "zh", "c")
NEAR = [(0, 1), (1, 0), (2, 3), (3, 2)]
NEXT = [(0, 3), (3, 0), (1, 2), (2, 1)]
ACROSS = [(0, 2), (2, 0), (1, 3), (3, 1)]
DOWN = [(0, 1), (2, 3)]
UP = [(1, 0), (3, 2)]
BACK = [(0, 3), (2, 1)]
BF = jnp.bfloat16
F32 = jnp.float32

LANES = 128
CHUNK = 256


def send(x, pairs):
    return lax.ppermute(x, "x", pairs)


def to_group(tiles):
    return lax.all_to_all(tiles, GROUP, split_axis=0, concat_axis=0, tiled=True)


def mul(a, b):
    return jnp.dot(a, b, preferred_element_type=F32)


def mul_t(a, b):
    return lax.dot_general(a, b, (((0,), (0,)), ((), ())), preferred_element_type=F32)


def call(kernel, outs, scratch, *args, flops=0):
    moved = sum(a.size * a.dtype.itemsize for a in args)
    space = pl.BlockSpec(memory_space=pltpu.VMEM)
    return pl.pallas_call(
        kernel,
        out_shape=[jax.ShapeDtypeStruct(s, d) for s, d in outs],
        in_specs=[
            pl.BlockSpec(memory_space=pltpu.SMEM) if a.dtype == jnp.int32 else space
            for a in args
        ],
        out_specs=[space] * len(outs),
        scratch_shapes=[pltpu.VMEM(s, d) for s, d in scratch],
        compiler_params=pltpu.CompilerParams(vmem_limit_bytes=16 << 20),
        cost_estimate=pl.CostEstimate(flops=flops, bytes_accessed=moved, transcendentals=0),
    )(*args)


def lower_mul(lower, vector, out):
    size = vector.shape[0]
    for first in range(0, size, CHUNK):
        last = min(first + CHUNK, size)
        out[first:last] = mul(lower[first:last, :last], vector[:last]).astype(out.dtype)


def lower_mul_t(lower, vector, out):
    size = vector.shape[0]
    for first in range(0, size, CHUNK):
        last = min(first + CHUNK, size)
        out[first:last] = mul_t(lower[first:, first:last], vector[first:]).astype(out.dtype)


def others(x):
    return x ^ 1, 3 - x, x ^ 2


def leaf_kernel(rows, loads_hbm, inv_hbm, coup_hbm, top, bot, loads, inv, coup, sems):
    copies = [
        pltpu.make_async_copy(src, dst, sems.at[n])
        for n, (src, dst) in enumerate(
            ((loads_hbm, loads), (inv_hbm, inv), (coup_hbm, coup))
        )
    ]
    for copy in copies:
        copy.start()
    copies[0].wait()
    copies[1].wait()
    fwd = mul(inv[...], loads[...]).astype(BF)
    copies[2].wait()
    half = top.shape[0]
    bot[...] = mul(coup[half:], fwd).astype(BF)
    top[...] = mul(coup[:half], fwd).astype(BF)


def leaf_call(rows, loads, inv, coup, half):
    args = [pltpu.with_memory_space_constraint(a, pltpu.HBM) for a in (loads, inv, coup)]
    ports = loads.shape[1]
    shape = jax.ShapeDtypeStruct((half, ports), BF)
    return pl.pallas_call(
        leaf_kernel,
        name="k_leaf",
        out_shape=[shape, shape],
        in_specs=[pl.BlockSpec(memory_space=pltpu.SMEM)]
        + [pl.BlockSpec(memory_space=pltpu.HBM)] * 3,
        out_specs=[pl.BlockSpec(memory_space=pltpu.VMEM)] * 2,
        scratch_shapes=[pltpu.VMEM(a.shape, a.dtype) for a in (loads, inv, coup)]
        + [pltpu.SemaphoreType.DMA((3,))],
        compiler_params=pltpu.CompilerParams(vmem_limit_bytes=8 << 20),
    )(rows, *args)


def first_kernel(at, inv, top, bot, came_top, came_bot, coup, came_coup, first, own, near, nxt, far, rhs, held, turned):
    x = at[0]
    high = x % 2
    half, sep = inv.shape
    ports = top.shape[1]
    width = held.shape[0]
    rhs[:half] = (-(top[...].astype(F32) + came_top[...].astype(F32))).astype(BF)
    rhs[half:] = (-(bot[...].astype(F32) + came_bot[...].astype(F32))).astype(BF)
    fwd = mul(inv[...], rhs[...]).astype(BF)
    first[...] = fwd
    pad = width - half
    held[:pad] = jnp.zeros((pad, ports), BF)
    held[half:] = jnp.zeros((pad, ports), BF)
    start = pl.multiple_of(high * pad, pad)
    held[pl.ds(start, half)] = fwd
    lane = pl.multiple_of(high * (sep - width), LANES)
    mine = coup[:, pl.ds(lane, width)]
    mine_at = pl.multiple_of(high * half, half)
    other_at = pl.multiple_of((1 - high) * half, half)
    share = own.shape[1]
    for at_col, who in enumerate((x,) + others(x)):
        cols = pl.ds(pl.multiple_of(who * share, LANES), share)
        turned[:, at_col * share : (at_col + 1) * share] = held[:, cols]
    for weights, row in ((mine, mine_at), (came_coup[...], other_at)):
        part = mul(weights, turned[...]).astype(BF)
        for at_col, ref in enumerate((own, near, nxt, far)):
            ref[pl.ds(row, half)] = part[:, at_col * share : (at_col + 1) * share]


def pack_kernel(at, inv, coup, fwd, pack):
    sep = inv.shape[1]
    rest = pack.shape[1] - sep - fwd.shape[1]
    start = pl.multiple_of((at[0] % 2) * (sep - rest), LANES)
    pack[:, :sep] = inv[...]
    pack[:, sep : sep + rest] = coup[:, pl.ds(start, rest)]
    pack[:, sep + rest :] = fwd[...]


def pieces(x, refs):
    return zip((x,) + others(x), refs)


def join_kernel(at, i0, i1, i2, i3, b0, up, nxt, down, inv, coup):
    x = at[0]
    each = i0.shape[0]
    for who, ref in pieces(x, (i0, i1, i2, i3)):
        inv[pl.ds(pl.multiple_of(who * each, each), each)] = ref[...]
    count = b0.shape[0]
    near = up[:count] + down[count:]
    far = up[count:] + down[:count]
    for who, block in pieces(x, (b0[...], near, nxt[...], far)):
        coup[pl.ds(pl.multiple_of(who * count, count), count)] = block


def second_kernel(rows, own, near, nxt, far, inv, coup, fwd, tiles, rhs):
    total = own[...].astype(F32) + near[...].astype(F32)
    total = total + (nxt[...].astype(F32) + far[...].astype(F32))
    rhs[...] = (-total).astype(BF)
    lower_mul(inv, rhs, fwd)
    for first in range(0, tiles.shape[0], CHUNK):
        part = mul(coup[first : first + CHUNK], fwd[...])
        live = lax.broadcasted_iota(jnp.int32, part.shape, 0) + first < rows[0]
        tiles[first : first + CHUNK] = jnp.where(live, part, 0.0).astype(BF)


def border_kernel(rows, rhs, inv, fwd, second, coup, back, mid, sol, diff):
    lower_mul(inv, rhs, mid)
    lower_mul_t(inv, mid, sol)
    live = lax.broadcasted_iota(jnp.int32, sol.shape, 0) < rows[0]
    masked = jnp.where(live, sol[...], 0.0).astype(BF)
    diff[...] = (fwd[...].astype(F32) - mul_t(coup[...], masked)).astype(BF)
    lower_mul_t(second, diff, back)


def fold_kernel(at, pack, came, coup, came_coup, leaf_coup, loads, leaf_inv, fold_t, inv_t, rest, full, fold):
    high = at[0] % 2
    half, sep = coup.shape
    width = came_coup.shape[1]
    mine_at = pl.multiple_of(high * half, half)
    other_at = pl.multiple_of((1 - high) * half, half)
    mine = mul(pack[:, :sep], leaf_coup[...]).astype(BF)
    other = mul(came[:, :sep], leaf_coup[...]).astype(BF)
    full[pl.ds(mine_at, half)] = mine
    full[pl.ds(other_at, half)] = other
    rest[...] = (
        mul(leaf_inv[...], loads[...]).astype(BF).astype(F32)
        - mul_t(mine, pack[:, sep + sep - width :])
        - mul_t(other, came[:, sep + sep - width :])
    )
    fold[pl.ds(mine_at, half)] = mul(coup[...], full[...]).astype(BF)
    win = pl.multiple_of(high * (sep - width), LANES)
    out = pl.multiple_of((1 - high) * width, LANES)
    fold[pl.ds(other_at, half)] = (
        mul(came_coup[...], full[pl.ds(win, width)])
        + mul(came[:, sep : sep + sep - width], full[pl.ds(out, sep - width)])
    ).astype(BF)
    fold_t[...] = fold[...].T
    inv_t[...] = leaf_inv[...].T


def most_kernel(at, fold_t, inv_t, rest, own, nxt, far, out, back, kept):
    x = at[0]
    share = own.shape[1]
    for place, (who, ref) in enumerate(zip((x, 3 - x, x ^ 2), (own, nxt, far))):
        spot = slice(place * share, (place + 1) * share)
        back[:, spot] = ref[...]
        kept[:, spot] = rest[:, pl.ds(pl.multiple_of(who * share, LANES), share)]
    diff = (kept[...] + mul(fold_t[...], back[...])).astype(BF)
    out[...] = mul(inv_t[...], diff).astype(BF)


def last_kernel(at, fold_t, inv_t, rest, near, most, out):
    x = at[0]
    share = near.shape[1]
    for place, who in enumerate((x, 3 - x, x ^ 2)):
        spot = slice(place * share, (place + 1) * share)
        out[:, pl.ds(pl.multiple_of(who * share, LANES), share)] = most[:, spot]
    cols = pl.ds(pl.multiple_of((x ^ 1) * share, LANES), share)
    diff = (rest[:, cols] + mul(fold_t[...], near[...])).astype(BF)
    out[:, cols] = mul(inv_t[...], diff).astype(BF)


def per_device(
    port_loads,
    leaf_inverse,
    leaf_coupling,
    first_inverse,
    second_coupling,
    second_inverse,
    border_coupling,
    border_inverse,
    border_rows,
):
    x = lax.axis_index("x")
    at = x.astype(jnp.int32)[None]
    low = x % 2 == 0
    group = lax.axis_size(GROUP)
    loads, leaf_inv, leaf_coup = port_loads[0, 0], leaf_inverse[0, 0], leaf_coupling[0, 0]
    inv_one, coup_two = first_inverse[0], second_coupling[0]
    half, sep = inv_one.shape
    leaf, ports = loads.shape
    share = ports // 4
    width = -(-half // LANES) * LANES
    border = border_inverse.shape[0]

    inv_two, coup_border = second_inverse[0], border_coupling[0]
    i_near = send(inv_two, NEAR)
    b_next = send(coup_border, NEXT)
    top, bot = leaf_call(border_rows, loads, leaf_inv, leaf_coup, half)
    came_bot = send(bot, DOWN)
    b_up = send(jnp.concatenate([coup_border, b_next], 0), UP)
    window = jnp.where(low, coup_two[:, sep - width :], coup_two[:, :width])
    came_coup = send(window, NEAR)
    came_top = send(top, NEAR)
    i_next = send(inv_two, NEXT)
    i_far = send(i_near, NEXT)
    b_down = send(b_up, BACK)
    quarter = ((sep, share), BF)
    fwd_one, own, near, nxt, far = call(
        first_kernel,
        [((half, ports), BF)] + [quarter] * 4,
        [((sep, ports), BF), ((width, ports), BF), ((width, ports), BF)],
        at,
        inv_one,
        top,
        bot,
        came_top,
        came_bot,
        coup_two,
        came_coup,
        flops=2 * half * ports * sep + 2 * sep * ports * width,
    )
    near = send(near, NEAR)
    far = send(far, ACROSS)
    nxt = send(nxt, NEXT)
    (pack,) = call(
        pack_kernel,
        [((half, 2 * sep - width + ports), BF)],
        [],
        at,
        inv_one,
        coup_two,
        fwd_one,
    )
    late_pack, near = lax.optimization_barrier((pack, near))
    came_pack = send(late_pack, NEAR)
    inv_full, coup_full = call(
        join_kernel,
        [((sep, sep), BF), ((border, sep), BF)],
        [],
        at,
        inv_two,
        i_near,
        i_next,
        i_far,
        coup_border,
        b_up,
        b_next,
        b_down,
    )
    fwd_two, tiles = call(
        second_kernel,
        [quarter, ((border, share), BF)],
        [quarter],
        border_rows,
        own,
        near,
        nxt,
        far,
        inv_full,
        coup_full,
        flops=2 * sep * share * (sep + border),
    )
    tiles = tiles.reshape(group, border // group, share)
    share_sum = jnp.sum(to_group(tiles).astype(F32), axis=0)
    rhs_share = (-share_sum).astype(BF)
    rhs_border = to_group(jnp.broadcast_to(rhs_share, tiles.shape)).reshape(border, share)
    (back_two,) = call(
        border_kernel,
        [quarter],
        [((border, share), BF), ((border, share), F32), quarter],
        border_rows,
        rhs_border,
        border_inverse,
        fwd_two,
        inv_full,
        coup_full,
        flops=2 * share * (2 * border * border + border * sep + sep * sep),
    )
    back_far = send(back_two, ACROSS)
    back_next = send(back_two, NEXT)
    back_near = send(back_two, NEAR)
    pack, came_pack, back_two = lax.optimization_barrier((pack, came_pack, back_two))
    fold_t, inv_t, rest = call(
        fold_kernel,
        [((leaf, sep), BF), ((leaf, leaf), BF), ((leaf, ports), F32)],
        [((sep, leaf), BF), ((sep, leaf), BF)],
        at,
        pack,
        came_pack,
        coup_two,
        came_coup,
        leaf_coup,
        loads,
        leaf_inv,
        flops=2 * sep * leaf * (2 * sep + ports),
    )
    (most,) = call(
        most_kernel,
        [((leaf, ports - share), BF)],
        [((sep, ports - share), BF), ((leaf, ports - share), F32)],
        at,
        fold_t,
        inv_t,
        rest,
        back_two,
        back_next,
        back_far,
        flops=2 * leaf * (ports - share) * (sep + leaf),
    )
    (out,) = call(
        last_kernel,
        [((leaf, ports), BF)],
        [],
        at,
        fold_t,
        inv_t,
        rest,
        back_near,
        most,
        flops=2 * leaf * share * (sep + leaf),
    )
    return out[None, None]


def solution(mesh):
    split = Mesh(mesh.devices.reshape(4, 4, 8, 2, 2), AXES)
    reg, sub = ("y", "zh", "c"), ("zl", "x")
    return jax.shard_map(
        per_device,
        mesh=split,
        in_specs=(P(reg, sub),) * 7 + (P(None, None), P(reg)),
        out_specs=P(reg, sub),
        check_vma=False,
    )
```

```python
import jax
import jax.numpy as jnp
from jax import lax
from jax.experimental import pallas as pl
from jax.experimental.pallas import tpu as pltpu
from jax.sharding import Mesh
from jax.sharding import PartitionSpec as P


AXES = ("zl", "x", "y", "zh", "c")
GROUP = ("zl", "y", "zh", "c")
NEAR = [(0, 1), (1, 0), (2, 3), (3, 2)]
NEXT = [(0, 3), (3, 0), (1, 2), (2, 1)]
ACROSS = [(0, 2), (2, 0), (1, 3), (3, 1)]
DOWN = [(0, 1), (2, 3)]
UP = [(1, 0), (3, 2)]
BACK = [(0, 3), (2, 1)]
BF = jnp.bfloat16
F32 = jnp.float32

LANES = 128
CHUNK = 256


def send(x, pairs):
    return lax.ppermute(x, "x", pairs)


def to_group(tiles):
    return lax.all_to_all(tiles, GROUP, split_axis=0, concat_axis=0, tiled=True)


def mul(a, b):
    return jnp.dot(a, b, preferred_element_type=F32)


def mul_t(a, b):
    return lax.dot_general(a, b, (((0,), (0,)), ((), ())), preferred_element_type=F32)


def call(kernel, outs, scratch, *args, flops=0):
    moved = sum(a.size * a.dtype.itemsize for a in args)
    space = pl.BlockSpec(memory_space=pltpu.VMEM)
    return pl.pallas_call(
        kernel,
        out_shape=[jax.ShapeDtypeStruct(s, d) for s, d in outs],
        in_specs=[
            pl.BlockSpec(memory_space=pltpu.SMEM) if a.dtype == jnp.int32 else space
            for a in args
        ],
        out_specs=[space] * len(outs),
        scratch_shapes=[pltpu.VMEM(s, d) for s, d in scratch],
        compiler_params=pltpu.CompilerParams(vmem_limit_bytes=16 << 20),
        cost_estimate=pl.CostEstimate(flops=flops, bytes_accessed=moved, transcendentals=0),
    )(*args)


def lower_mul(lower, vector, out):
    size = vector.shape[0]
    for first in range(0, size, CHUNK):
        last = min(first + CHUNK, size)
        out[first:last] = mul(lower[first:last, :last], vector[:last]).astype(out.dtype)


def others(x):
    return x ^ 1, 3 - x, x ^ 2


def leaf_kernel(rows, loads_hbm, inv_hbm, coup_hbm, top, bot, loads, inv, coup, sems):
    copies = [
        pltpu.make_async_copy(src, dst, sems.at[n])
        for n, (src, dst) in enumerate(
            ((loads_hbm, loads), (inv_hbm, inv), (coup_hbm, coup))
        )
    ]
    for copy in copies:
        copy.start()
    copies[0].wait()
    copies[1].wait()
    fwd = mul(inv[...], loads[...]).astype(BF)
    copies[2].wait()
    half = top.shape[0]
    bot[...] = mul(coup[half:], fwd).astype(BF)
    top[...] = mul(coup[:half], fwd).astype(BF)


def leaf_call(rows, loads, inv, coup, half):
    args = [pltpu.with_memory_space_constraint(a, pltpu.HBM) for a in (loads, inv, coup)]
    ports = loads.shape[1]
    shape = jax.ShapeDtypeStruct((half, ports), BF)
    return pl.pallas_call(
        leaf_kernel,
        name="k_leaf",
        out_shape=[shape, shape],
        in_specs=[pl.BlockSpec(memory_space=pltpu.SMEM)]
        + [pl.BlockSpec(memory_space=pltpu.HBM)] * 3,
        out_specs=[pl.BlockSpec(memory_space=pltpu.VMEM)] * 2,
        scratch_shapes=[pltpu.VMEM(a.shape, a.dtype) for a in (loads, inv, coup)]
        + [pltpu.SemaphoreType.DMA((3,))],
        compiler_params=pltpu.CompilerParams(vmem_limit_bytes=8 << 20),
    )(rows, *args)


def pre_kernel(inv, bot, came, part, rhs):
    pad = rhs.shape[0] - bot.shape[0]
    rhs[:pad] = jnp.zeros((pad, rhs.shape[1]), BF)
    rhs[pad:] = (-(bot[...].astype(F32) + came[...].astype(F32))).astype(BF)
    part[...] = mul(inv[:, inv.shape[1] - rhs.shape[0] :], rhs[...])


def first_kernel(at, inv, part, top, came_top, coup, came_coup, first, own, near, nxt, far, rhs, held, turned):
    x = at[0]
    high = x % 2
    half, sep = inv.shape
    ports = top.shape[1]
    width = held.shape[0]
    rhs[:half] = (-(top[...].astype(F32) + came_top[...].astype(F32))).astype(BF)
    rhs[half:] = jnp.zeros((width - half, ports), BF)
    fwd = (part[...] + mul(inv[:, :width], rhs[...])).astype(BF)
    first[...] = fwd
    pad = width - half
    held[:pad] = jnp.zeros((pad, ports), BF)
    held[half:] = jnp.zeros((pad, ports), BF)
    start = pl.multiple_of(high * pad, pad)
    held[pl.ds(start, half)] = fwd
    lane = pl.multiple_of(high * (sep - width), LANES)
    mine = coup[:, pl.ds(lane, width)]
    mine_at = pl.multiple_of(high * half, half)
    other_at = pl.multiple_of((1 - high) * half, half)
    share = own.shape[1]
    for at_col, who in enumerate((x,) + others(x)):
        cols = pl.ds(pl.multiple_of(who * share, LANES), share)
        turned[:, at_col * share : (at_col + 1) * share] = held[:, cols]
    for weights, row in ((mine, mine_at), (came_coup[...], other_at)):
        part = mul(weights, turned[...]).astype(BF)
        for at_col, ref in enumerate((own, near, nxt, far)):
            ref[pl.ds(row, half)] = part[:, at_col * share : (at_col + 1) * share]


def pack_kernel(at, inv, coup, fwd, pack):
    sep = inv.shape[1]
    rest = pack.shape[1] - sep - fwd.shape[1]
    start = pl.multiple_of((at[0] % 2) * (sep - rest), LANES)
    pack[:, :sep] = inv[...]
    pack[:, sep : sep + rest] = coup[:, pl.ds(start, rest)]
    pack[:, sep + rest :] = fwd[...]


def pieces(x, refs):
    return zip((x,) + others(x), refs)


def join_kernel(at, rows, i0, i1, i2, i3, b0, up, nxt, down, border, inv, coup, fold):
    x = at[0]
    each = i0.shape[0]
    for who, ref in pieces(x, (i0, i1, i2, i3)):
        inv[pl.ds(pl.multiple_of(who * each, each), each)] = ref[...]
    count = b0.shape[0]
    near = up[:count] + down[count:]
    far = up[count:] + down[:count]
    for who, block in pieces(x, (b0[...], near, nxt[...], far)):
        first = pl.multiple_of(who * count, count)
        live = lax.broadcasted_iota(jnp.int32, block.shape, 0) + first < rows[0]
        coup[pl.ds(first, count)] = jnp.where(live, block.astype(F32), 0.0).astype(BF)
    both = mul_t(border[...], border[...]).astype(BF)
    down_two = mul_t(coup[...], both).astype(BF)
    fold[...] = mul_t(inv[...], down_two).astype(BF)


def second_kernel(own, near, nxt, far, inv, coup, fwd, tiles, rhs):
    total = own[...].astype(F32) + near[...].astype(F32)
    total = total + (nxt[...].astype(F32) + far[...].astype(F32))
    rhs[...] = (-total).astype(BF)
    lower_mul(inv, rhs, fwd)
    for first in range(0, tiles.shape[0], CHUNK):
        tiles[first : first + CHUNK] = mul(coup[first : first + CHUNK], fwd[...]).astype(BF)


def border_kernel(rhs, fwd, second, fold, back):
    size = fwd.shape[0]
    for first in range(0, size, CHUNK):
        last = min(first + CHUNK, size)
        local = mul_t(second[first:, first:last], fwd[first:])
        back[first:last] = (local - mul(fold[first:last], rhs[...])).astype(BF)


def fold_kernel(at, pack, came, coup, came_coup, leaf_coup, loads, leaf_inv, fold_t, inv_t, rest, full, fold):
    high = at[0] % 2
    half, sep = coup.shape
    width = came_coup.shape[1]
    mine_at = pl.multiple_of(high * half, half)
    other_at = pl.multiple_of((1 - high) * half, half)
    mine = mul(pack[:, :sep], leaf_coup[...]).astype(BF)
    other = mul(came[:, :sep], leaf_coup[...]).astype(BF)
    full[pl.ds(mine_at, half)] = mine
    full[pl.ds(other_at, half)] = other
    rest[...] = (
        mul(leaf_inv[...], loads[...]).astype(BF).astype(F32)
        - mul_t(mine, pack[:, sep + sep - width :])
        - mul_t(other, came[:, sep + sep - width :])
    )
    fold[pl.ds(mine_at, half)] = mul(coup[...], full[...]).astype(BF)
    win = pl.multiple_of(high * (sep - width), LANES)
    out = pl.multiple_of((1 - high) * width, LANES)
    fold[pl.ds(other_at, half)] = (
        mul(came_coup[...], full[pl.ds(win, width)])
        + mul(came[:, sep : sep + sep - width], full[pl.ds(out, sep - width)])
    ).astype(BF)
    fold_t[...] = fold[...].T
    inv_t[...] = leaf_inv[...].T


def most_kernel(at, fold_t, inv_t, rest, own, nxt, far, out, back, kept):
    x = at[0]
    share = own.shape[1]
    for place, (who, ref) in enumerate(zip((x, 3 - x, x ^ 2), (own, nxt, far))):
        spot = slice(place * share, (place + 1) * share)
        back[:, spot] = ref[...]
        kept[:, spot] = rest[:, pl.ds(pl.multiple_of(who * share, LANES), share)]
    diff = (kept[...] + mul(fold_t[...], back[...])).astype(BF)
    out[...] = mul(inv_t[...], diff).astype(BF)


def last_kernel(at, fold_t, inv_t, rest, near, most, out):
    x = at[0]
    share = near.shape[1]
    for place, who in enumerate((x, 3 - x, x ^ 2)):
        spot = slice(place * share, (place + 1) * share)
        out[:, pl.ds(pl.multiple_of(who * share, LANES), share)] = most[:, spot]
    cols = pl.ds(pl.multiple_of((x ^ 1) * share, LANES), share)
    diff = (rest[:, cols] + mul(fold_t[...], near[...])).astype(BF)
    out[:, cols] = mul(inv_t[...], diff).astype(BF)


def per_device(
    port_loads,
    leaf_inverse,
    leaf_coupling,
    first_inverse,
    second_coupling,
    second_inverse,
    border_coupling,
    border_inverse,
    border_rows,
):
    x = lax.axis_index("x")
    at = x.astype(jnp.int32)[None]
    low = x % 2 == 0
    group = lax.axis_size(GROUP)
    loads, leaf_inv, leaf_coup = port_loads[0, 0], leaf_inverse[0, 0], leaf_coupling[0, 0]
    inv_one, coup_two = first_inverse[0], second_coupling[0]
    half, sep = inv_one.shape
    leaf, ports = loads.shape
    share = ports // 4
    width = -(-half // LANES) * LANES
    border = border_inverse.shape[0]

    inv_two, coup_border = second_inverse[0], border_coupling[0]
    i_near = send(inv_two, NEAR)
    b_next = send(coup_border, NEXT)
    top, bot = leaf_call(border_rows, loads, leaf_inv, leaf_coup, half)
    came_bot = send(bot, DOWN)
    b_up = send(jnp.concatenate([coup_border, b_next], 0), UP)
    window = jnp.where(low, coup_two[:, sep - width :], coup_two[:, :width])
    came_coup = send(window, NEAR)
    came_top = send(top, NEAR)
    i_next = send(inv_two, NEXT)
    i_far = send(i_near, NEXT)
    b_down = send(b_up, BACK)
    quarter = ((sep, share), BF)
    (part_one,) = call(
        pre_kernel,
        [((half, ports), F32)],
        [((width, ports), BF)],
        inv_one,
        bot,
        came_bot,
        flops=2 * half * ports * width,
    )
    fwd_one, own, near, nxt, far = call(
        first_kernel,
        [((half, ports), BF)] + [quarter] * 4,
        [((width, ports), BF)] * 3,
        at,
        inv_one,
        part_one,
        top,
        came_top,
        coup_two,
        came_coup,
        flops=2 * half * ports * sep + 2 * sep * ports * width,
    )
    near = send(near, NEAR)
    far = send(far, ACROSS)
    nxt = send(nxt, NEXT)
    (pack,) = call(
        pack_kernel,
        [((half, 2 * sep - width + ports), BF)],
        [],
        at,
        inv_one,
        coup_two,
        fwd_one,
    )
    late_pack, near = lax.optimization_barrier((pack, near))
    came_pack = send(late_pack, NEAR)
    inv_full, coup_full, border_fold = call(
        join_kernel,
        [((sep, sep), BF), ((border, sep), BF), ((sep, border), BF)],
        [],
        at,
        border_rows,
        inv_two,
        i_near,
        i_next,
        i_far,
        coup_border,
        b_up,
        b_next,
        b_down,
        border_inverse,
    )
    fwd_two, tiles = call(
        second_kernel,
        [quarter, ((border, share), BF)],
        [quarter],
        own,
        near,
        nxt,
        far,
        inv_full,
        coup_full,
        flops=2 * sep * share * (sep + border),
    )
    tiles = tiles.reshape(group, border // group, share)
    share_sum = jnp.sum(to_group(tiles).astype(F32), axis=0)
    rhs_share = (-share_sum).astype(BF)
    rhs_border = to_group(jnp.broadcast_to(rhs_share, tiles.shape)).reshape(border, share)
    (back_two,) = call(
        border_kernel,
        [quarter],
        [],
        rhs_border,
        fwd_two,
        inv_full,
        border_fold,
        flops=2 * share * (border * sep + sep * sep),
    )
    back_far = send(back_two, ACROSS)
    back_next = send(back_two, NEXT)
    back_near = send(back_two, NEAR)
    pack, came_pack, back_two = lax.optimization_barrier((pack, came_pack, back_two))
    fold_t, inv_t, rest = call(
        fold_kernel,
        [((leaf, sep), BF), ((leaf, leaf), BF), ((leaf, ports), F32)],
        [((sep, leaf), BF), ((sep, leaf), BF)],
        at,
        pack,
        came_pack,
        coup_two,
        came_coup,
        leaf_coup,
        loads,
        leaf_inv,
        flops=2 * sep * leaf * (2 * sep + ports),
    )
    (most,) = call(
        most_kernel,
        [((leaf, ports - share), BF)],
        [((sep, ports - share), BF), ((leaf, ports - share), F32)],
        at,
        fold_t,
        inv_t,
        rest,
        back_two,
        back_next,
        back_far,
        flops=2 * leaf * (ports - share) * (sep + leaf),
    )
    (out,) = call(
        last_kernel,
        [((leaf, ports), BF)],
        [],
        at,
        fold_t,
        inv_t,
        rest,
        back_near,
        most,
        flops=2 * leaf * share * (sep + leaf),
    )
    return out[None, None]


def solution(mesh):
    split = Mesh(mesh.devices.reshape(4, 4, 8, 2, 2), AXES)
    reg, sub = ("y", "zh", "c"), ("zl", "x")
    return jax.shard_map(
        per_device,
        mesh=split,
        in_specs=(P(reg, sub),) * 7 + (P(None, None), P(reg)),
        out_specs=P(reg, sub),
        check_vma=False,
    )
```

```python
import jax
import jax.numpy as jnp
from jax import lax
from jax.experimental import pallas as pl
from jax.experimental.pallas import tpu as pltpu
from jax.sharding import Mesh
from jax.sharding import PartitionSpec as P


AXES = ("zl", "x", "y", "zh", "c")
GROUP = ("zl", "y", "zh", "c")
NEAR = [(0, 1), (1, 0), (2, 3), (3, 2)]
NEXT = [(0, 3), (3, 0), (1, 2), (2, 1)]
ACROSS = [(0, 2), (2, 0), (1, 3), (3, 1)]
DOWN = [(0, 1), (2, 3)]
UP = [(1, 0), (3, 2)]
BACK = [(0, 3), (2, 1)]
BF = jnp.bfloat16
F32 = jnp.float32

LANES = 128
CHUNK = 256


def send(x, pairs):
    return lax.ppermute(x, "x", pairs)


def to_group(tiles):
    return lax.all_to_all(tiles, GROUP, split_axis=0, concat_axis=0, tiled=True)


def mul(a, b):
    return jnp.dot(a, b, preferred_element_type=F32)


def mul_t(a, b):
    return lax.dot_general(a, b, (((0,), (0,)), ((), ())), preferred_element_type=F32)


def call(kernel, outs, scratch, *args, flops=0):
    moved = sum(a.size * a.dtype.itemsize for a in args)
    space = pl.BlockSpec(memory_space=pltpu.VMEM)
    return pl.pallas_call(
        kernel,
        out_shape=[jax.ShapeDtypeStruct(s, d) for s, d in outs],
        in_specs=[
            pl.BlockSpec(memory_space=pltpu.SMEM) if a.dtype == jnp.int32 else space
            for a in args
        ],
        out_specs=[space] * len(outs),
        scratch_shapes=[pltpu.VMEM(s, d) for s, d in scratch],
        compiler_params=pltpu.CompilerParams(vmem_limit_bytes=16 << 20),
        cost_estimate=pl.CostEstimate(flops=flops, bytes_accessed=moved, transcendentals=0),
    )(*args)


def lower_mul(lower, vector, out):
    size = vector.shape[0]
    for first in range(0, size, CHUNK):
        last = min(first + CHUNK, size)
        out[first:last] = mul(lower[first:last, :last], vector[:last]).astype(out.dtype)


def others(x):
    return x ^ 1, 3 - x, x ^ 2


def leaf_kernel(rows, loads_hbm, inv_hbm, coup_hbm, top, bot, loads, inv, coup, sems):
    copies = [
        pltpu.make_async_copy(src, dst, sems.at[n])
        for n, (src, dst) in enumerate(
            ((loads_hbm, loads), (inv_hbm, inv), (coup_hbm, coup))
        )
    ]
    for copy in copies:
        copy.start()
    copies[0].wait()
    copies[1].wait()
    fwd = mul(inv[...], loads[...]).astype(BF)
    copies[2].wait()
    half = top.shape[0]
    bot[...] = mul(coup[half:], fwd).astype(BF)
    top[...] = mul(coup[:half], fwd).astype(BF)


def leaf_call(rows, loads, inv, coup, half):
    args = [pltpu.with_memory_space_constraint(a, pltpu.HBM) for a in (loads, inv, coup)]
    ports = loads.shape[1]
    shape = jax.ShapeDtypeStruct((half, ports), BF)
    return pl.pallas_call(
        leaf_kernel,
        name="k_leaf",
        out_shape=[shape, shape],
        in_specs=[pl.BlockSpec(memory_space=pltpu.SMEM)]
        + [pl.BlockSpec(memory_space=pltpu.HBM)] * 3,
        out_specs=[pl.BlockSpec(memory_space=pltpu.VMEM)] * 2,
        scratch_shapes=[pltpu.VMEM(a.shape, a.dtype) for a in (loads, inv, coup)]
        + [pltpu.SemaphoreType.DMA((3,))],
        compiler_params=pltpu.CompilerParams(vmem_limit_bytes=8 << 20),
    )(rows, *args)


def pre_kernel(inv, bot, came, part, rhs):
    pad = rhs.shape[0] - bot.shape[0]
    rhs[:pad] = jnp.zeros((pad, rhs.shape[1]), BF)
    rhs[pad:] = (-(bot[...].astype(F32) + came[...].astype(F32))).astype(BF)
    part[...] = mul(inv[:, inv.shape[1] - rhs.shape[0] :], rhs[...])


def first_kernel(at, inv, part, top, came_top, coup, came_coup, first, own, near, nxt, far, rhs, held, turned):
    x = at[0]
    high = x % 2
    half, sep = inv.shape
    ports = top.shape[1]
    width = held.shape[0]
    rhs[:half] = (-(top[...].astype(F32) + came_top[...].astype(F32))).astype(BF)
    rhs[half:] = jnp.zeros((width - half, ports), BF)
    fwd = (part[...] + mul(inv[:, :width], rhs[...])).astype(BF)
    first[...] = fwd
    pad = width - half
    held[:pad] = jnp.zeros((pad, ports), BF)
    held[half:] = jnp.zeros((pad, ports), BF)
    start = pl.multiple_of(high * pad, pad)
    held[pl.ds(start, half)] = fwd
    lane = pl.multiple_of(high * (sep - width), LANES)
    mine = coup[:, pl.ds(lane, width)]
    mine_at = pl.multiple_of(high * half, half)
    other_at = pl.multiple_of((1 - high) * half, half)
    share = own.shape[1]
    for at_col, who in enumerate((x,) + others(x)):
        cols = pl.ds(pl.multiple_of(who * share, LANES), share)
        turned[:, at_col * share : (at_col + 1) * share] = held[:, cols]
    for weights, row in ((mine, mine_at), (came_coup[...], other_at)):
        part = mul(weights, turned[...]).astype(BF)
        for at_col, ref in enumerate((own, near, nxt, far)):
            ref[pl.ds(row, half)] = part[:, at_col * share : (at_col + 1) * share]


def pack_kernel(at, inv, coup, fwd, pack):
    sep = inv.shape[1]
    rest = pack.shape[1] - sep - fwd.shape[1]
    start = pl.multiple_of((at[0] % 2) * (sep - rest), LANES)
    pack[:, :sep] = inv[...]
    pack[:, sep : sep + rest] = coup[:, pl.ds(start, rest)]
    pack[:, sep + rest :] = fwd[...]


def pieces(x, refs):
    return zip((x,) + others(x), refs)


def join_kernel(at, rows, i0, i1, i2, i3, b0, up, nxt, down, border, inv, coup, fold):
    x = at[0]
    each = i0.shape[0]
    for who, ref in pieces(x, (i0, i1, i2, i3)):
        inv[pl.ds(pl.multiple_of(who * each, each), each)] = ref[...]
    count = b0.shape[0]
    near = up[:count] + down[count:]
    far = up[count:] + down[:count]
    for who, block in pieces(x, (b0[...], near, nxt[...], far)):
        first = pl.multiple_of(who * count, count)
        live = lax.broadcasted_iota(jnp.int32, block.shape, 0) + first < rows[0]
        coup[pl.ds(first, count)] = jnp.where(live, block.astype(F32), 0.0).astype(BF)
    both = mul_t(border[...], border[...]).astype(BF)
    down_two = mul_t(coup[...], both).astype(BF)
    fold[...] = mul_t(inv[...], down_two).astype(BF)


def second_kernel(own, near, nxt, far, inv, coup, fwd, tiles, rhs):
    total = own[...].astype(F32) + near[...].astype(F32)
    total = total + (nxt[...].astype(F32) + far[...].astype(F32))
    rhs[...] = (-total).astype(BF)
    lower_mul(inv, rhs, fwd)
    for first in range(0, tiles.shape[0], CHUNK):
        tiles[first : first + CHUNK] = mul(coup[first : first + CHUNK], fwd[...]).astype(BF)


def border_kernel(rhs, fwd, second, fold, back):
    size = fwd.shape[0]
    for first in range(0, size, CHUNK):
        last = min(first + CHUNK, size)
        local = mul_t(second[first:, first:last], fwd[first:])
        back[first:last] = (local - mul(fold[first:last], rhs[...])).astype(BF)


def fold_kernel(at, pack, came, coup, came_coup, leaf_coup, loads, leaf_inv, fold_t, inv_t, rest, full, fold):
    high = at[0] % 2
    half, sep = coup.shape
    width = came_coup.shape[1]
    mine_at = pl.multiple_of(high * half, half)
    other_at = pl.multiple_of((1 - high) * half, half)
    mine = mul(pack[:, :sep], leaf_coup[...]).astype(BF)
    other = mul(came[:, :sep], leaf_coup[...]).astype(BF)
    full[pl.ds(mine_at, half)] = mine
    full[pl.ds(other_at, half)] = other
    rest[...] = (
        mul(leaf_inv[...], loads[...]).astype(BF).astype(F32)
        - mul_t(mine, pack[:, sep + sep - width :])
        - mul_t(other, came[:, sep + sep - width :])
    )
    fold[pl.ds(mine_at, half)] = mul(coup[...], full[...]).astype(BF)
    win = pl.multiple_of(high * (sep - width), LANES)
    out = pl.multiple_of((1 - high) * width, LANES)
    fold[pl.ds(other_at, half)] = (
        mul(came_coup[...], full[pl.ds(win, width)])
        + mul(came[:, sep : sep + sep - width], full[pl.ds(out, sep - width)])
    ).astype(BF)
    fold_t[...] = fold[...].T
    inv_t[...] = leaf_inv[...].T


def most_kernel(at, fold_t, inv_t, rest, own, nxt, far, out, back, kept, done, sems):
    x = at[0]
    share = own.shape[1]
    owners = (x, 3 - x, x ^ 2)
    for place, (who, ref) in enumerate(zip(owners, (own, nxt, far))):
        spot = slice(place * share, (place + 1) * share)
        back[:, spot] = ref[...]
        kept[:, spot] = rest[:, pl.ds(pl.multiple_of(who * share, LANES), share)]
    diff = (kept[...] + mul(fold_t[...], back[...])).astype(BF)
    done[...] = mul(inv_t[...], diff).astype(BF)
    copies = [
        pltpu.make_async_copy(
            done.at[:, place * share : (place + 1) * share],
            out.at[:, pl.ds(pl.multiple_of(who * share, LANES), share)],
            sems.at[place],
        )
        for place, who in enumerate(owners)
    ]
    for copy in copies:
        copy.start()
    for copy in copies:
        copy.wait()


def last_kernel(at, fold_t, inv_t, rest, near, most, out, done, sem):
    share = near.shape[1]
    cols = pl.ds(pl.multiple_of((at[0] ^ 1) * share, LANES), share)
    diff = (rest[:, cols] + mul(fold_t[...], near[...])).astype(BF)
    done[...] = mul(inv_t[...], diff).astype(BF)
    copy = pltpu.make_async_copy(done, out.at[:, cols], sem)
    copy.start()
    copy.wait()


def solve_call(kernel, shape, scratch, aliases, *args):
    vmem, hbm = pl.BlockSpec(memory_space=pltpu.VMEM), pl.BlockSpec(memory_space=pltpu.HBM)
    specs = [pl.BlockSpec(memory_space=pltpu.SMEM)] + [vmem] * (len(args) - 1)
    for operand in aliases:
        specs[operand] = hbm
    return pl.pallas_call(
        kernel,
        out_shape=pltpu.HBM(shape, BF),
        in_specs=specs,
        out_specs=hbm,
        scratch_shapes=scratch,
        input_output_aliases=aliases,
        compiler_params=pltpu.CompilerParams(vmem_limit_bytes=16 << 20),
    )(*args)


def per_device(
    port_loads,
    leaf_inverse,
    leaf_coupling,
    first_inverse,
    second_coupling,
    second_inverse,
    border_coupling,
    border_inverse,
    border_rows,
):
    x = lax.axis_index("x")
    at = x.astype(jnp.int32)[None]
    low = x % 2 == 0
    group = lax.axis_size(GROUP)
    loads, leaf_inv, leaf_coup = port_loads[0, 0], leaf_inverse[0, 0], leaf_coupling[0, 0]
    inv_one, coup_two = first_inverse[0], second_coupling[0]
    half, sep = inv_one.shape
    leaf, ports = loads.shape
    share = ports // 4
    width = -(-half // LANES) * LANES
    border = border_inverse.shape[0]

    inv_two, coup_border = second_inverse[0], border_coupling[0]
    i_near = send(inv_two, NEAR)
    b_next = send(coup_border, NEXT)
    top, bot = leaf_call(border_rows, loads, leaf_inv, leaf_coup, half)
    came_bot = send(bot, DOWN)
    b_up = send(jnp.concatenate([coup_border, b_next], 0), UP)
    window = jnp.where(low, coup_two[:, sep - width :], coup_two[:, :width])
    came_coup = send(window, NEAR)
    came_top = send(top, NEAR)
    i_next = send(inv_two, NEXT)
    i_far = send(i_near, NEXT)
    b_down = send(b_up, BACK)
    quarter = ((sep, share), BF)
    (part_one,) = call(
        pre_kernel,
        [((half, ports), F32)],
        [((width, ports), BF)],
        inv_one,
        bot,
        came_bot,
        flops=2 * half * ports * width,
    )
    fwd_one, own, near, nxt, far = call(
        first_kernel,
        [((half, ports), BF)] + [quarter] * 4,
        [((width, ports), BF)] * 3,
        at,
        inv_one,
        part_one,
        top,
        came_top,
        coup_two,
        came_coup,
        flops=2 * half * ports * sep + 2 * sep * ports * width,
    )
    near = send(near, NEAR)
    far = send(far, ACROSS)
    nxt = send(nxt, NEXT)
    (pack,) = call(
        pack_kernel,
        [((half, 2 * sep - width + ports), BF)],
        [],
        at,
        inv_one,
        coup_two,
        fwd_one,
    )
    late_pack, near = lax.optimization_barrier((pack, near))
    came_pack = send(late_pack, NEAR)
    inv_full, coup_full, border_fold = call(
        join_kernel,
        [((sep, sep), BF), ((border, sep), BF), ((sep, border), BF)],
        [],
        at,
        border_rows,
        inv_two,
        i_near,
        i_next,
        i_far,
        coup_border,
        b_up,
        b_next,
        b_down,
        border_inverse,
    )
    fwd_two, tiles = call(
        second_kernel,
        [quarter, ((border, share), BF)],
        [quarter],
        own,
        near,
        nxt,
        far,
        inv_full,
        coup_full,
        flops=2 * sep * share * (sep + border),
    )
    tiles = tiles.reshape(group, border // group, share)
    share_sum = jnp.sum(to_group(tiles).astype(F32), axis=0)
    rhs_share = (-share_sum).astype(BF)
    rhs_border = to_group(jnp.broadcast_to(rhs_share, tiles.shape)).reshape(border, share)
    (back_two,) = call(
        border_kernel,
        [quarter],
        [],
        rhs_border,
        fwd_two,
        inv_full,
        border_fold,
        flops=2 * share * (border * sep + sep * sep),
    )
    back_far = send(back_two, ACROSS)
    back_next = send(back_two, NEXT)
    back_near = send(back_two, NEAR)
    pack, came_pack, back_two = lax.optimization_barrier((pack, came_pack, back_two))
    fold_t, inv_t, rest = call(
        fold_kernel,
        [((leaf, sep), BF), ((leaf, leaf), BF), ((leaf, ports), F32)],
        [((sep, leaf), BF), ((sep, leaf), BF)],
        at,
        pack,
        came_pack,
        coup_two,
        came_coup,
        leaf_coup,
        loads,
        leaf_inv,
        flops=2 * sep * leaf * (2 * sep + ports),
    )
    kept = ports - share
    most = solve_call(
        most_kernel,
        (leaf, ports),
        [
            pltpu.VMEM((sep, kept), BF),
            pltpu.VMEM((leaf, kept), F32),
            pltpu.VMEM((leaf, kept), BF),
            pltpu.SemaphoreType.DMA((3,)),
        ],
        {},
        at,
        fold_t,
        inv_t,
        rest,
        back_two,
        back_next,
        back_far,
    )
    out = solve_call(
        last_kernel,
        (leaf, ports),
        [pltpu.VMEM((leaf, share), BF), pltpu.SemaphoreType.DMA(())],
        {5: 0},
        at,
        fold_t,
        inv_t,
        rest,
        back_near,
        most,
    )
    return out[None, None]


def solution(mesh):
    split = Mesh(mesh.devices.reshape(4, 4, 8, 2, 2), AXES)
    reg, sub = ("y", "zh", "c"), ("zl", "x")
    return jax.shard_map(
        per_device,
        mesh=split,
        in_specs=(P(reg, sub),) * 7 + (P(None, None), P(reg)),
        out_specs=P(reg, sub),
        check_vma=False,
    )
```
